512 devices in a mesh: seq: 16 (over y, x), expert: 32 (over z, core).
Axes of the slice: x: 4, y: 4, z: 16, core: 2. Of those that a mesh axis runs over, the one named last changes fastest.
Arguments:
- tokens: bfloat16 [8192, 2048], P(('seq', 'expert')), may hold values from -6 to 6
- out_grads: bfloat16 [8192, 2048], P(('seq', 'expert')), may hold values from -6 to 6
- route_ids: int32 [8192, 6], P(('seq', 'expert')), may hold values from 0 to 63, all different within a row; in each aligned block of 16 rows (0 to 15, 16 to 31, ...) at most 2 rows name the same one
- route_probs: bfloat16 [8192, 6], P(('seq', 'expert')), may hold values from 0.049804688 to 1
- w_gate_up: bfloat16 [512, 2, 176, 2048], P(('seq', 'expert')), may hold values from -0.125 to 0.125
- w_down: bfloat16 [512, 176, 2048], P(('seq', 'expert')), may hold values from -0.15625 to 0.15625
Outputs:
- grad_tokens: bfloat16 [8192, 2048], P(('seq', 'expert'))
- grad_probs: float32 [8192, 6], P(('seq', 'expert'))
- grad_gate_up: bfloat16 [512, 2, 176, 2048], P(('seq', 'expert'))
- grad_down: bfloat16 [512, 176, 2048], P(('seq', 'expert'))
The draws below stay inside these ranges and needn't reach their ends.
Inputs may be any that keep to these rules, and one draw needn't show every extreme that they name: `route_ids`: in the rows of one device (16 aligned rows) no expert is named by more than 2 routes, a bound that some block reaches; a token's 6 experts differ.
All inputs are finite; a program needn't handle non-finite values.
Results may differ from the reference program's by a relative error of at most 0.0065.
Values may be sent and summed in bfloat16 or wider, within the bound.
A program may use at most 64 MiB of HBM per device.

```python
import math
import jax
import jax.numpy as jnp
import numpy as np
from jax import lax

D = 2048
FF = 1408
TOP = 6
TOK_DEV = 16
SLICES = 8
HID_DEV = 176
EXPERTS = 64
CAP = 2
TOKENS = 8192


def block_levels(own_key, extent, shards, least, largest):
    def one(axis_at, parts):
        draws = jax.random.uniform(jax.random.fold_in(jax.random.fold_in(own_key, 6), axis_at), (parts,), jnp.float32, least / len(shards), largest / len(shards))
        return jnp.repeat(jnp.exp(draws), extent[axis_at] // parts).reshape((-1,) + (1,) * (len(extent) - axis_at - 1))

    factor_of = one(*shards[0])
    for cut in shards[1:]:
        factor_of = factor_of * one(*cut)
    return factor_of


def routed_block(rng, own, number, rows, count, top, limit, lean):
    sequence = jax.random.permutation(rng, count)
    crowded, ordinary = shares(count, rows * top, limit, lean, True), shares(count, rows * top, limit, lean, False)
    places = jnp.arange(count)

    def named(sizes, turn):
        used = int((sizes > 0).sum())
        fixed = max(1, used // 4)
        shifted = fixed + (places - fixed + turn * (used - fixed)) % max(1, count - fixed)
        return jnp.zeros((count,), jnp.int32).at[sequence[jnp.where(places < fixed, places, shifted)]].set(jnp.asarray(sizes, jnp.int32))

    sizes = jnp.where(number % 4 == 0, named(crowded, number // 4), named(ordinary, number - number // 4 - 1))
    mixed = jax.random.permutation(jax.random.fold_in(own, 3), count)
    giver, sink = mixed[0:count // 2 * 2:2], mixed[1:count // 2 * 2:2]
    margin = jnp.minimum(sizes[giver] - 1, limit - sizes[sink]) // 2
    margin = jnp.where((giver == sequence[0]) | (sink == sequence[0]) | (sizes[sink] == 0), 0, jnp.maximum(margin, 0))
    shifted = jax.random.randint(jax.random.fold_in(own, 4), (count // 2,), 0, 1 << 20) % (margin + 1)
    sizes = sizes.at[giver].add(-shifted).at[sink].add(shifted)
    items = jnp.searchsorted(jnp.cumsum(sizes), jnp.arange(rows * top), side="right").astype(jnp.int32)
    listing = items.reshape(top, rows).T
    listing = listing[jax.random.permutation(jax.random.fold_in(own, 1), rows)]
    turn = jax.random.randint(jax.random.fold_in(own, 2), (rows, 1), 0, top)
    return jnp.take_along_axis(listing, (jnp.arange(top)[None, :] + turn) % top, axis=1)


def shares(number_of, total, most, skew, full):
    portions = [(1 << 20) // math.isqrt(standing ** skew) + 1 for standing in range(1, number_of + 1)]
    largest = most if full else min(most, max(-(-total // number_of), total * portions[0] // sum(portions)))
    least = 1 if total - largest >= number_of - 1 else 0
    given, surplus = [largest] + [least] * (number_of - 1), total - largest - least * (number_of - 1)
    while surplus > 0:
        free = [i for i in range(1, number_of) if given[i] < largest] or [i for i in range(1, number_of) if given[i] < most]
        whole, remaining = sum([portions[i] for i in free]), surplus
        for i in free:
            more = min(most - given[i], max(1, remaining * portions[i] // whole), surplus)
            given[i] = given[i] + more
            surplus = surplus - more
    return np.array(given)


def normal_values(key, shape, spread, bound, pieces=(), kind=jnp.bfloat16):
    loudness = block_levels(key, shape, pieces, -0.22, 0.18) if pieces else 1.0
    entries = jax.random.normal(key, shape, jnp.float32) * spread * loudness
    return jnp.minimum(jnp.maximum(entries, -bound), bound).astype(kind)


def setup_inputs(seed: int = 0) -> dict:
    streams_of = jax.random.split(jax.random.key(seed), 7)
    tokens = normal_values(streams_of[0], (TOKENS, D), 1.0, 6.0, ((0, 512),))
    out_grads = normal_values(streams_of[1], (TOKENS, D), 1.0, 6.0, ((0, 512),))
    route_ids_keys = jax.random.split(jax.random.fold_in(streams_of[2], 1), TOKENS // TOK_DEV)
    route_ids_turns = jax.random.permutation(jax.random.fold_in(streams_of[2], 3), TOKENS // TOK_DEV)
    route_ids = jax.vmap(lambda own, number: routed_block(jax.random.fold_in(streams_of[2], 2), own, number, TOK_DEV, EXPERTS, TOP, CAP, 2))(route_ids_keys, route_ids_turns).reshape((TOKENS, TOP))
    route_probs = jnp.clip(jnp.exp(math.log(1.0) - 2.9996462 * jax.random.uniform(streams_of[3], (TOKENS, TOP), jnp.float32) ** block_levels(streams_of[3], (TOKENS, TOP), ((0, 512),), -0.2, 0.2)), 0.049804688, 1.0).astype(jnp.bfloat16)
    w_gate_up = normal_values(streams_of[4], (EXPERTS * SLICES, 2, HID_DEV, D), D ** -0.5, 0.125, ((0, 512),))
    w_down = normal_values(streams_of[5], (EXPERTS * SLICES, HID_DEV, D), FF ** -0.5, 0.15625, ((0, 512),))
    return dict(tokens=tokens, out_grads=out_grads, route_ids=route_ids, route_probs=route_probs, w_gate_up=w_gate_up, w_down=w_down)


def slot_numbers(route_ids):
    nrows = route_ids.shape[0]
    blocks = nrows // TOK_DEV
    flat = route_ids.reshape(blocks, TOK_DEV * TOP)
    onehot = (flat[:, :, None] == jnp.arange(EXPERTS, dtype=jnp.int32)[None, None, :]).astype(jnp.int32)
    before = jnp.cumsum(onehot, axis=1) - onehot
    rank = jnp.sum(before * onehot, axis=2)
    slot = jnp.arange(blocks, dtype=jnp.int32)[:, None] * CAP + rank
    return slot.reshape(nrows, TOP).astype(jnp.int32)


def rounded(value):
    return lax.optimization_barrier(value.astype(jnp.bfloat16)).astype(jnp.float32)


def reference(tokens, out_grads, route_ids, route_probs, w_gate_up, w_down):
    nrows = tokens.shape[0]
    nroutes = nrows * TOP
    slot = slot_numbers(route_ids)
    slots_all = (nrows // TOK_DEV) * CAP
    table = jnp.full((EXPERTS, slots_all), nroutes, dtype=jnp.int32)
    table = table.at[route_ids.reshape(-1), slot.reshape(-1)].set(jnp.arange(nroutes, dtype=jnp.int32))
    tokens_pad = jnp.concatenate([tokens, jnp.zeros((1, D), tokens.dtype)], 0)
    grads_pad = jnp.concatenate([out_grads, jnp.zeros((1, D), out_grads.dtype)], 0)
    probs_pad = jnp.concatenate([route_probs.reshape(-1), jnp.zeros((1,), route_probs.dtype)], 0)
    gate_up_all = w_gate_up.reshape(EXPERTS, SLICES, 2, HID_DEV, D)
    down_all = w_down.reshape(EXPERTS, SLICES, HID_DEV, D)

    def expert_grads(packed):
        index, gate_up, down = packed
        token = (index // TOP).astype(jnp.int32)
        xs = tokens_pad[token]
        dys = grads_pad[token]
        weight = probs_pad[index].astype(jnp.float32)[:, None]
        scaled = (weight * dys.astype(jnp.float32)).astype(jnp.bfloat16)
        dx_total = jnp.zeros((slots_all, D), jnp.float32)
        score_total = jnp.zeros((slots_all,), jnp.float32)
        gate_parts, up_parts, down_parts = [], [], []
        for part in range(SLICES):
            w_gate = gate_up[part, 0]
            w_up = gate_up[part, 1]
            w_out = down[part]
            gate = jnp.dot(xs, w_gate.T, preferred_element_type=jnp.float32)
            upper = jnp.dot(xs, w_up.T, preferred_element_type=jnp.float32)
            sig = jax.nn.sigmoid(gate)
            act = gate * sig * upper
            err = jnp.dot(dys, w_out.T, preferred_element_type=jnp.float32)
            score_total = score_total + rounded(jnp.sum(err * act, axis=1))
            delta = weight * err
            grad_g = (delta * upper * sig * (1.0 + gate * (1.0 - sig))).astype(jnp.bfloat16)
            grad_u = (delta * gate * sig).astype(jnp.bfloat16)
            dx_part = jnp.dot(grad_g, w_gate, preferred_element_type=jnp.float32) + jnp.dot(grad_u, w_up, preferred_element_type=jnp.float32)
            dx_total = dx_total + rounded(dx_part)
            gate_parts.append(jnp.dot(grad_g.T, xs, preferred_element_type=jnp.float32).astype(jnp.bfloat16))
            up_parts.append(jnp.dot(grad_u.T, xs, preferred_element_type=jnp.float32).astype(jnp.bfloat16))
            down_parts.append(jnp.dot(act.astype(jnp.bfloat16).T, scaled, preferred_element_type=jnp.float32).astype(jnp.bfloat16))
        grad_gu = jnp.stack([jnp.stack(gate_parts, 0), jnp.stack(up_parts, 0)], 1)
        return dx_total.astype(jnp.bfloat16), score_total.astype(jnp.bfloat16), grad_gu, jnp.stack(down_parts, 0)

    slot_dx, slot_score, grad_gate_up, grad_down = lax.map(expert_grads, (table, gate_up_all, down_all))
    total = jnp.zeros((nrows, D), jnp.float32)
    for pick in range(TOP):
        total = total + slot_dx[route_ids[:, pick], slot[:, pick]].astype(jnp.float32)
    grad_probs = slot_score[route_ids, slot].astype(jnp.float32)
    grad_gate_up = grad_gate_up.reshape(EXPERTS * SLICES, 2, HID_DEV, D)
    grad_down = grad_down.reshape(EXPERTS * SLICES, HID_DEV, D)
    return total.astype(jnp.bfloat16), grad_probs, grad_gate_up, grad_down
```

```python
import functools

import jax
import jax.numpy as jnp
from jax import lax
from jax.experimental import pallas as pl
from jax.experimental.pallas import tpu as pltpu
from jax.sharding import PartitionSpec as P

MESH = pl.DeviceIdType.MESH
CAP = 2
EXTRA = 128
BF = jnp.bfloat16
F32 = jnp.float32


def dot(a, b, ca, cb):
    return lax.dot_general(a, b, (((ca,), (cb,)), ((), ())), preferred_element_type=F32)


def tiles(width, size):
    return [(at, min(size, width - at)) for at in range(0, width, size)]


def kernel(
    G,
    Z,
    top,
    tok_ref,
    og_ref,
    meta_ref,
    wgu_hbm,
    wd_hbm,
    gt_ref,
    gp_ref,
    ggu_hbm,
    gd_hbm,
    xm,
    dyb,
    sbuf,
    rbuf,
    pt,
    wgu,
    wd,
    ggt,
    actt,
    dxo,
    dxs,
    dxr,
    rts,
    rtr,
    tp,
    rss,
    rsr,
    ggu,
    gd,
    ag_send,
    ag_recv,
    ip_send,
    ip_recv,
    sw_send,
    sw_recv,
    dx_send,
    dx_recv,
    rt_send,
    rt_recv,
    rs_send,
    rs_recv,
    w_sem,
    o_sem,
):
    B, D = tok_ref.shape
    H = wd.shape[0]
    W2 = D + EXTRA
    half = Z // 2
    quarter = Z // 4
    R = half * CAP
    rows = G * R
    nt = half * B
    side = 4 if G == 16 else 0

    s = lax.axis_index("seq")
    e = lax.axis_index("expert")
    z = e // 2
    c = e % 2
    q = e // (Z * 2 // 4)
    expert = s * 4 + q
    right = lax.rem(z + 1, Z) * 2 + c
    left = lax.rem(z + Z - 1, Z) * 2 + c
    partner = z * 2 + 1 - c

    def ahead(i):
        if side:
            return lax.rem(s // side + i // side, side) * side + lax.rem(s % side + i % side, side)
        return lax.rem(s + i, G)

    def behind(i):
        if side:
            return lax.rem(s // side + side - i // side, side) * side + lax.rem(
                s % side + side - i % side, side
            )
        return lax.rem(s + G - i, G)

    def loop(lo, hi, fn):
        def step(i, carry):
            fn(i)
            return carry

        lax.fori_loop(lo, hi, step, 0)

    w_copies = [
        pltpu.make_async_copy(wgu_hbm.at[0], wgu, w_sem.at[0]),
        pltpu.make_async_copy(wd_hbm.at[0], wd, w_sem.at[1]),
    ]
    for copy in w_copies:
        copy.start()

    barrier = pltpu.get_barrier_semaphore()

    def greet(i):
        pl.semaphore_signal(barrier, inc=1, device_id=(ahead(i), e), device_id_type=MESH)

    loop(1, G, greet)
    for other in (right, left, partner):
        pl.semaphore_signal(barrier, inc=1, device_id=(s, other), device_id_type=MESH)

    def pos(rel):
        return lax.rem(rel + quarter + 2 * Z, Z)

    own = quarter
    xm[own, :, :D] = tok_ref[...]
    xm[own, :, D:] = meta_ref[...]
    dyb[own] = og_ref[...]

    pl.semaphore_wait(barrier, G - 1 + 3)

    def ag(way, i, piece):
        buf = xm if piece == 0 else dyb
        src, dst = (pos(-i), pos(-i - 1)) if way == 0 else (pos(i), pos(i + 1))
        return pltpu.make_async_remote_copy(
            src_ref=buf.at[src],
            dst_ref=buf.at[dst],
            send_sem=ag_send.at[way, piece, i],
            recv_sem=ag_recv.at[way, piece, i],
            device_id=(s, right if way == 0 else left),
            device_id_type=MESH,
        )

    def ag_step(i):
        for piece in range(2):
            for way in range(2):
                ag(way, i - 1, piece).wait_recv()
                ag(way, i, piece).start()

    def ag_last():
        for piece in range(2):
            for way in range(2):
                ag(way, half - 2, piece).wait_recv()
            ag(0, half - 1, piece).start()

    def ip(ch, piece, to, frm):
        return pltpu.make_async_remote_copy(
            src_ref=sbuf.at[ch, piece, pl.ds(to * R, R)],
            dst_ref=rbuf.at[c, ch, piece, pl.ds(frm * R, R)],
            send_sem=ip_send.at[ch, piece, to],
            recv_sem=ip_recv.at[ch, piece, frm],
            device_id=(to, e),
            device_id_type=MESH,
        )

    def ip_own(ch, piece):
        return pltpu.make_async_copy(
            sbuf.at[ch, piece, pl.ds(s * R, R)],
            rbuf.at[c, ch, piece, pl.ds(s * R, R)],
            ip_send.at[ch, piece, s],
        )

    def iota(shape, dim):
        return lax.broadcasted_iota(jnp.int32, shape, dim)

    def log2(n):
        return n.bit_length() - 1

    def pick(ch):
        blocks = pl.ds(ch * half, half)
        meta = xm[blocks, :, D:].reshape(nt, EXTRA).astype(F32)
        lane_expert = (iota((nt, EXTRA), 1) * 4 + q).astype(F32)
        member = jnp.zeros((nt, EXTRA), F32)
        weight = jnp.zeros((nt, EXTRA), F32)
        for k in range(top):
            hit = jnp.broadcast_to(meta[:, k : k + 1], (nt, EXTRA)) == lane_expert
            member = member + jnp.where(hit, 1.0, 0.0)
            weight = weight + jnp.where(
                hit, jnp.broadcast_to(meta[:, 8 + k : 9 + k], (nt, EXTRA)), 0.0
            )
        member = member.astype(BF)
        weight = weight.astype(BF)
        ti, tj = iota((nt, nt), 0), iota((nt, nt), 1)
        earlier = ((ti >> log2(B)) == (tj >> log2(B))) & (tj < ti)
        rank = dot(jnp.where(earlier, 1.0, 0.0).astype(BF), member, 1, 0).astype(BF)
        spread = jnp.where(
            iota((EXTRA, rows), 0) == (iota((EXTRA, rows), 1) >> log2(R)), 1.0, 0.0
        ).astype(BF)
        member_s = dot(member, spread, 1, 0)
        rank_s = dot(rank, spread, 1, 0)
        weight_s = dot(weight, spread, 1, 0)
        tok, slot = iota((nt, rows), 0), iota((nt, rows), 1)
        mine = (tok >> log2(B)) == ((slot & (R - 1)) >> 1)
        chosen = (member_s > 0.5) & (rank_s == (slot & 1).astype(F32)) & mine
        picked = jnp.where(chosen, 1.0, 0.0).astype(BF)
        pt[ch] = picked
        for piece in range(2):
            matrix = picked if piece == 0 else jnp.where(chosen, weight_s, 0.0).astype(BF)
            for at, wide in tiles(D, 512):
                if piece == 0:
                    block = xm[blocks, :, at : at + wide].reshape(nt, wide)
                else:
                    block = dyb[blocks, :, at : at + wide].reshape(nt, wide)
                sbuf[ch, piece, :, at : at + wide] = dot(matrix, block, 0, 0).astype(BF)
            loop(1, G, lambda i: ip(ch, piece, ahead(i), s).start())
            ip_own(ch, piece).start()

    for piece in range(2):
        for way in range(2):
            ag(way, 0, piece).start()
    if quarter < half - 1:
        loop(1, quarter + 1, ag_step)
        pick(0)
        loop(quarter + 1, half - 1, ag_step)
        ag_last()
    else:
        loop(1, half - 1, ag_step)
        ag_last()
        pick(0)
    for piece in range(2):
        ag(0, half - 1, piece).wait_recv()
    pick(1)

    def sw(ch, piece, frm, core):
        return pltpu.make_async_remote_copy(
            src_ref=rbuf.at[core, ch, piece, pl.ds(frm * R, R)],
            dst_ref=rbuf.at[core, ch, piece, pl.ds(frm * R, R)],
            send_sem=sw_send.at[ch, piece, frm],
            recv_sem=sw_recv.at[ch, piece, frm],
            device_id=(s, partner),
            device_id_type=MESH,
        )

    def swap(ch, piece):
        ip_own(ch, piece).wait()
        sw(ch, piece, s, c).start()

        def forward(i):
            frm = behind(i)
            ip(ch, piece, frm, frm).wait_recv()
            sw(ch, piece, frm, c).start()

        loop(1, G, forward)

    def swapped(ch, piece):
        loop(0, G, lambda i: sw(ch, piece, i, 1 - c).wait_recv())

    def forward_part(ch, core, unit):
        x = rbuf[core, ch, 0]
        gu = dot(wgu[...].reshape(2 * H, D), x, 1, 1)
        gate, upper = gu[:H], gu[H:]
        err = dot(wd[...], rbuf[core, ch, 1], 1, 1)
        sig = jax.nn.sigmoid(gate)
        act = gate * sig * upper
        actt[unit] = act.astype(BF)
        ggt[unit, :H] = (err * upper * sig * (1.0 + gate * (1.0 - sig))).astype(BF)
        ggt[unit, H:] = (err * gate * sig).astype(BF)
        score = jnp.sum(err * act, axis=0, keepdims=True)
        score = jnp.broadcast_to(score, (16, rows)).astype(BF)
        mark = (iota((16, EXTRA), 0) == 0) & (iota((16, EXTRA), 1) == expert)
        return dot(score, jnp.where(mark, 1.0, 0.0).astype(BF), 0, 0)

    def dx_part(unit, put):
        for at, wide in tiles(D, 512):
            w = wgu[:, :, at : at + wide].reshape(2 * H, wide)
            put(at, wide, dot(ggt[unit], w, 0, 0))

    def dx_copy(ch):
        return pltpu.make_async_remote_copy(
            src_ref=dxs.at[ch],
            dst_ref=dxr.at[ch],
            send_sem=dx_send.at[ch],
            recv_sem=dx_recv.at[ch],
            device_id=(s, partner),
            device_id_type=MESH,
        )

    def rt(ch, to, frm):
        return pltpu.make_async_remote_copy(
            src_ref=rts.at[ch, pl.ds(to * R, R)],
            dst_ref=rtr.at[ch, pl.ds(frm * R, R)],
            send_sem=rt_send.at[ch, to],
            recv_sem=rt_recv.at[ch, frm],
            device_id=(to, e),
            device_id_type=MESH,
        )

    def rt_own(ch):
        return pltpu.make_async_copy(
            rts.at[ch, pl.ds(s * R, R)], rtr.at[ch, pl.ds(s * R, R)], rt_send.at[ch, s]
        )

    def compute(ch):
        def put_other(at, wide, value):
            dxs[ch, :, at : at + wide] = value.astype(BF)

        def put_own(at, wide, value):
            dxo[:, at : at + wide] = value

        put_other(D, EXTRA, forward_part(ch, 1 - c, 2 * ch))
        dx_part(2 * ch, put_other)
        dx_copy(ch).start()
        put_own(D, EXTRA, forward_part(ch, c, 2 * ch + 1))
        dx_part(2 * ch + 1, put_own)
        dx_copy(ch).wait_recv()
        for at, wide in tiles(W2, 512):
            cols = slice(at, at + wide)
            rts[ch, :, cols] = (dxo[:, cols] + dxr[ch, :, cols].astype(F32)).astype(BF)
        loop(1, G, lambda i: rt(ch, ahead(i), s).start())
        rt_own(ch).start()

    for piece in range(2):
        swap(0, piece)
    for copy in w_copies:
        copy.wait()
    for piece in range(2):
        swapped(0, piece)
    compute(0)
    for piece in range(2):
        swap(1, piece)
    for piece in range(2):
        swapped(1, piece)
    compute(1)

    for at, wide in tiles(D, 512):
        cols = slice(at, at + wide)
        total = jnp.zeros((2 * H, wide), F32)
        total_down = jnp.zeros((H, wide), F32)
        for unit in range(4):
            core = (1 - c) if unit % 2 == 0 else c
            total = total + dot(ggt[unit], rbuf[core, unit // 2, 0, :, cols], 1, 0)
            total_down = total_down + dot(actt[unit], rbuf[core, unit // 2, 1, :, cols], 1, 0)
        ggu[:, :, cols] = total.astype(BF).reshape(2, H, wide)
        gd[:, cols] = total_down.astype(BF)
    o_copies = [
        pltpu.make_async_copy(ggu, ggu_hbm.at[0], o_sem.at[0]),
        pltpu.make_async_copy(gd, gd_hbm.at[0], o_sem.at[1]),
    ]
    for copy in o_copies:
        copy.start()

    for ch in range(2):
        rt_own(ch).wait()

        def back(i):
            frm = behind(i)
            rt(ch, frm, frm).wait_recv()

        loop(1, G, back)
        for at, wide in tiles(W2, 512):
            value = dot(pt[ch], rtr[ch, :, at : at + wide], 1, 0)
            tp[ch * half : (ch + 1) * half, :, at : at + wide] = value.reshape(half, B, wide)

    def rs(way, i):
        return pltpu.make_async_remote_copy(
            src_ref=rss.at[way, i],
            dst_ref=rsr.at[way, i],
            send_sem=rs_send.at[way, i],
            recv_sem=rs_recv.at[way, i],
            device_id=(s, right if way == 0 else left),
            device_id_type=MESH,
        )

    def rs_rel(way, i):
        return half - i if way == 0 else -(half - 1 - i)

    for way in range(2):
        rss[way, 0] = tp[pos(rs_rel(way, 0))].astype(BF)
        rs(way, 0).start()

    def rs_step(i, ways=(0, 1)):
        for way in ways:
            rs(way, i - 1).wait_recv()
            rss[way, i] = (tp[pos(rs_rel(way, i))] + rsr[way, i - 1].astype(F32)).astype(BF)
            rs(way, i).start()

    loop(1, half - 1, rs_step)
    rs_step(half - 1, (0,))
    rs(1, half - 2).wait_recv()
    rs(0, half - 1).wait_recv()
    total = tp[own] + rsr[0, half - 1].astype(F32) + rsr[1, half - 2].astype(F32)
    gt_ref[...] = total[:, :D].astype(BF)
    scores = total[:, D:]
    meta = meta_ref[...].astype(F32)
    lane = iota((B, EXTRA), 1).astype(F32)
    for k in range(top):
        hit = jnp.broadcast_to(meta[:, k : k + 1], (B, EXTRA)) == lane
        value = jnp.sum(jnp.where(hit, scores, 0.0), axis=1, keepdims=True)
        gp_ref[:, k : k + 1] = value / meta[:, 8 + k : 9 + k]

    for piece in range(2):
        loop(0, half - 1, lambda i: ag(0, i, piece).wait_send())
        loop(0, half - 1, lambda i: ag(1, i, piece).wait_send())
        ag(0, half - 1, piece).wait_send()
    for ch in range(2):
        for piece in range(2):
            loop(1, G, lambda i: ip(ch, piece, ahead(i), s).wait_send())
            loop(0, G, lambda i: sw(ch, piece, i, c).wait_send())
        dx_copy(ch).wait_send()
        loop(1, G, lambda i: rt(ch, ahead(i), s).wait_send())
    loop(0, half - 1, lambda i: rs(0, i).wait_send())
    loop(0, half - 1, lambda i: rs(1, i).wait_send())
    rs(0, half - 1).wait_send()
    for copy in o_copies:
        copy.wait()


def body(tokens, out_grads, route_ids, route_probs, w_gate_up, w_down):
    B, D = tokens.shape
    top = route_ids.shape[1]
    H = w_down.shape[1]
    G = lax.axis_size("seq")
    Z = lax.axis_size("expert") // 2
    half = Z // 2
    R = half * CAP
    rows = G * R
    nt = half * B
    W2 = D + EXTRA
    meta = jnp.concatenate(
        [
            route_ids.astype(BF),
            jnp.zeros((B, 8 - top), BF),
            route_probs,
            jnp.zeros((B, EXTRA - 8 - top), BF),
        ],
        axis=1,
    )
    vmem = pl.BlockSpec(memory_space=pltpu.VMEM)
    anys = pl.BlockSpec(memory_space=pl.ANY)
    dma = pltpu.SemaphoreType.DMA
    gt, gp, ggu, gd = pl.pallas_call(
        functools.partial(kernel, G, Z, top),
        out_shape=(
            jax.ShapeDtypeStruct((B, D), BF),
            jax.ShapeDtypeStruct((B, top), F32),
            jax.ShapeDtypeStruct(w_gate_up.shape, BF),
            jax.ShapeDtypeStruct(w_down.shape, BF),
        ),
        in_specs=[vmem, vmem, vmem, anys, anys],
        out_specs=(vmem, vmem, anys, anys),
        scratch_shapes=[
            pltpu.VMEM((Z, B, W2), BF),
            pltpu.VMEM((Z, B, D), BF),
            pltpu.VMEM((2, 2, rows, D), BF),
            pltpu.VMEM((2, 2, 2, rows, D), BF),
            pltpu.VMEM((2, nt, rows), BF),
            pltpu.VMEM((2, H, D), BF),
            pltpu.VMEM((H, D), BF),
            pltpu.VMEM((4, 2 * H, rows), BF),
            pltpu.VMEM((4, H, rows), BF),
            pltpu.VMEM((rows, W2), F32),
            pltpu.VMEM((2, rows, W2), BF),
            pltpu.VMEM((2, rows, W2), BF),
            pltpu.VMEM((2, rows, W2), BF),
            pltpu.VMEM((2, rows, W2), BF),
            pltpu.VMEM((Z, B, W2), F32),
            pltpu.VMEM((2, half, B, W2), BF),
            pltpu.VMEM((2, half, B, W2), BF),
            pltpu.VMEM((2, H, D), BF),
            pltpu.VMEM((H, D), BF),
            dma((2, 2, half)),
            dma((2, 2, half)),
            dma((2, 2, G)),
            dma((2, 2, G)),
            dma((2, 2, G)),
            dma((2, 2, G)),
            dma((2,)),
            dma((2,)),
            dma((2, G)),
            dma((2, G)),
            dma((2, half)),
            dma((2, half)),
            dma((2,)),
            dma((2,)),
        ],
        compiler_params=pltpu.CompilerParams(
            collective_id=0, has_side_effects=True, vmem_limit_bytes=56 * 1024 * 1024
        ),
        name="moe_backward",
    )(tokens, out_grads, meta, w_gate_up, w_down)
    return gt, gp, ggu, gd


def solution(mesh):
    in_specs = (
        P(("seq", "expert"), None),
        P(("seq", "expert"), None),
        P(("seq", "expert"), None),
        P(("seq", "expert"), None),
        P(("seq", "expert"), None, None, None),
        P(("seq", "expert"), None, None),
    )
    out_specs = (
        P(("seq", "expert"), None),
        P(("seq", "expert"), None),
        P(("seq", "expert"), None, None, None),
        P(("seq", "expert"), None, None),
    )
    return jax.shard_map(body, mesh=mesh, in_specs=in_specs, out_specs=out_specs, check_vma=False)
```

```python
import functools

import jax
import jax.numpy as jnp
from jax import lax
from jax.experimental import pallas as pl
from jax.experimental.pallas import tpu as pltpu
from jax.sharding import PartitionSpec as P

MESH = pl.DeviceIdType.MESH
CAP = 2
EXTRA = 128
BF = jnp.bfloat16
F32 = jnp.float32


def dot(a, b, ca, cb):
    return lax.dot_general(a, b, (((ca,), (cb,)), ((), ())), preferred_element_type=F32)


def tiles(width, size):
    return [(at, min(size, width - at)) for at in range(0, width, size)]


BLOCKS = (-2, -1, 0, 1, -4, -3, 2, 3, -6, -5, 4, 5, -8, -7, 6, 7)
POS = {rel: at for at, rel in enumerate(BLOCKS)}
NEAR = (-4, 3, -3, 2, -2, 1, -1)
FAR = ((1, 6, 0), (2, 7, 0), (-1, 4, 0), (1, -5, 1), (-1, -7, 1), (-2, -8, 1))
LAST = ((5, 5), (-6, -6))
GREET = (-3, -2, -1, 1, 2, 3, 4, -5, 6)


def kernel(
    G,
    Z,
    top,
    pieces,
    tok_ref,
    og_ref,
    ids_ref,
    probs_ref,
    wgu_hbm,
    wd_hbm,
    gt_ref,
    gp_ref,
    ggu_hbm,
    gd_hbm,
    xm,
    dyb,
    sbuf,
    rbuf,
    pt,
    wgu,
    wd,
    ggt,
    actt,
    rts,
    rtr,
    tp,
    nrs,
    nrr,
    frs,
    frr,
    lrs,
    lrr,
    wg_own,
    wg_snd,
    wg_rcv,
    ggu,
    gd,
    ag_send,
    ag_recv,
    ip_send,
    ip_recv,
    rt_send,
    rt_recv,
    nr_send,
    nr_recv,
    fr_send,
    fr_recv,
    lr_send,
    lr_recv,
    wx_send,
    wx_recv,
    w_sem,
    o_sem,
):
    B, D = tok_ref.shape
    H = wd.shape[1]
    W2 = D + EXTRA
    half = Z // 2
    quarter = Z // 4
    R = quarter * CAP
    rows = G * R
    nt = quarter * B
    side = 4 if G == 16 else 0

    s = lax.axis_index("seq")
    e = lax.axis_index("expert")
    z = e // 2
    c = e % 2
    q = e // (Z * 2 // 4)
    expert = s * 4 + q
    partner = (s, z * 2 + 1 - c)

    def along(k):
        return (s, lax.rem(z + Z + k, Z) * 2 + c)

    def ahead(i):
        if side:
            return lax.rem(s // side + i // side, side) * side + lax.rem(s % side + i % side, side)
        return lax.rem(s + i, G)

    def behind(i):
        if side:
            return lax.rem(s // side + side - i // side, side) * side + lax.rem(
                s % side + side - i % side, side
            )
        return lax.rem(s + G - i, G)

    def loop(lo, hi, fn):
        def step(i, carry):
            fn(i)
            return carry

        lax.fori_loop(lo, hi, step, 0)

    def iota(shape, dim):
        return lax.broadcasted_iota(jnp.int32, shape, dim)

    def log2(n):
        return n.bit_length() - 1

    def remote(src, dst, send, recv, to):
        return pltpu.make_async_remote_copy(
            src_ref=src,
            dst_ref=dst,
            send_sem=send,
            recv_sem=recv,
            device_id=to,
            device_id_type=MESH,
        )

    w_copies = [
        pltpu.make_async_copy(wgu_hbm.at[0], wgu.at[c], w_sem.at[0]),
        pltpu.make_async_copy(wd_hbm.at[0], wd.at[c], w_sem.at[1]),
    ]
    for copy in w_copies:
        copy.start()

    barrier = pltpu.get_barrier_semaphore()

    def greet(i):
        pl.semaphore_signal(barrier, inc=1, device_id=(ahead(i), e), device_id_type=MESH)

    loop(1, G, greet)
    for k in GREET:
        pl.semaphore_signal(barrier, inc=1, device_id=along(k), device_id_type=MESH)
    pl.semaphore_signal(barrier, inc=1, device_id=partner, device_id_type=MESH)

    lane = iota((B, EXTRA), 1)
    ids = ids_ref[...].astype(F32)
    probs = probs_ref[...].astype(F32)
    own_meta = jnp.zeros((B, EXTRA), F32)
    for k in range(top):
        own_meta = jnp.where(
            lane == k, jnp.broadcast_to(ids[:, k : k + 1], (B, EXTRA)), own_meta
        )
        own_meta = jnp.where(
            lane == 8 + k, jnp.broadcast_to(probs[:, k : k + 1], (B, EXTRA)), own_meta
        )
    own = POS[0]
    xm[own, :, :D] = tok_ref[...]
    xm[own, :, D:] = own_meta.astype(BF)
    dyb[own] = og_ref[...]

    pl.semaphore_wait(barrier, G - 1 + len(GREET) + 1)

    def ag(way, i, piece):
        buf = xm if piece == 0 else dyb
        src, dst = (-i, -i - 1) if way == 0 else (i, i + 1)
        return remote(
            buf.at[POS[src]],
            buf.at[POS[dst]],
            ag_send.at[way, piece, i],
            ag_recv.at[way, piece, i],
            along(1 if way == 0 else -1),
        )

    last = (half - 1, half - 2)

    def ag_step(i):
        for piece in range(2):
            for way in range(2):
                if 0 <= i - 1 <= last[way]:
                    ag(way, i - 1, piece).wait_recv()
                if i <= last[way]:
                    ag(way, i, piece).start()

    def wx(i):
        src = wgu if i == 0 else wd
        return remote(src.at[c], src.at[c], wx_send.at[i], wx_recv.at[i], partner)

    def wx_in(i):
        src = wgu if i == 0 else wd
        return remote(src.at[1 - c], src.at[1 - c], wx_send.at[i], wx_recv.at[i], partner)

    def ip(n, piece, to, frm):
        return remote(
            sbuf.at[n // 2, piece, n % 2, pl.ds(to * R, R)],
            rbuf.at[n // 2, piece, n % 2, pl.ds(frm * R, R)],
            ip_send.at[n, piece, to],
            ip_recv.at[n, piece, frm],
            (to, e),
        )

    def ip_own(n, piece):
        return pltpu.make_async_copy(
            sbuf.at[n // 2, piece, n % 2, pl.ds(s * R, R)],
            rbuf.at[n // 2, piece, n % 2, pl.ds(s * R, R)],
            ip_send.at[n, piece, s],
        )

    def pick(n):
        blocks = pl.ds(n * quarter, quarter)
        meta = xm[blocks, :, D:].reshape(nt, EXTRA).astype(F32)
        lane_expert = (iota((nt, EXTRA), 1) * 4 + q).astype(F32)
        member = jnp.zeros((nt, EXTRA), F32)
        weight = jnp.zeros((nt, EXTRA), F32)
        for k in range(top):
            hit = jnp.broadcast_to(meta[:, k : k + 1], (nt, EXTRA)) == lane_expert
            member = member + jnp.where(hit, 1.0, 0.0)
            weight = weight + jnp.where(
                hit, jnp.broadcast_to(meta[:, 8 + k : 9 + k], (nt, EXTRA)), 0.0
            )
        member = member.astype(BF)
        weight = weight.astype(BF)
        ti, tj = iota((nt, nt), 0), iota((nt, nt), 1)
        earlier = ((ti >> log2(B)) == (tj >> log2(B))) & (tj < ti)
        rank = dot(jnp.where(earlier, 1.0, 0.0).astype(BF), member, 1, 0).astype(BF)
        spread = jnp.where(
            iota((EXTRA, rows), 0) == (iota((EXTRA, rows), 1) >> log2(R)), 1.0, 0.0
        ).astype(BF)
        member_s = dot(member, spread, 1, 0)
        rank_s = dot(rank, spread, 1, 0)
        weight_s = dot(weight, spread, 1, 0)
        tok, slot = iota((nt, rows), 0), iota((nt, rows), 1)
        mine = (tok >> log2(B)) == ((slot & (R - 1)) >> 1)
        chosen = (member_s > 0.5) & (rank_s == (slot & 1).astype(F32)) & mine
        picked = jnp.where(chosen, 1.0, 0.0).astype(BF)
        pt[n] = picked
        for piece in range(2):
            matrix = picked if piece == 0 else jnp.where(chosen, weight_s, 0.0).astype(BF)
            for at, wide in tiles(D, 512):
                if piece == 0:
                    block = xm[blocks, :, at : at + wide].reshape(nt, wide)
                else:
                    block = dyb[blocks, :, at : at + wide].reshape(nt, wide)
                value = dot(matrix, block, 0, 0).astype(BF)
                sbuf[n // 2, piece, n % 2, :, at : at + wide] = value
            loop(1, G, lambda i: ip(n, piece, ahead(i), s).start())
            ip_own(n, piece).start()

    ag_step(0)
    for copy in w_copies:
        copy.wait()
    for i in range(2):
        wx(i).start()
    for n in range(4):
        ag_step(2 * n + 1)
        ag_step(2 * n + 2)
        pick(n)

    def arrived(n):
        for piece in range(2):
            ip_own(n, piece).wait()

            def one(i):
                frm = behind(i)
                ip(n, piece, frm, frm).wait_recv()

            loop(1, G, one)

    def forward_part(ch):
        x = rbuf[ch, 0].reshape(2 * rows, D)
        dy = rbuf[ch, 1].reshape(2 * rows, D)
        score = jnp.zeros((1, 2 * rows), F32)
        for k in range(2):
            gu = dot(wgu[k].reshape(2 * H, D), x, 1, 1)
            gate, upper = gu[:H], gu[H:]
            err = dot(wd[k], dy, 1, 1)
            sig = jax.nn.sigmoid(gate)
            act = gate * sig * upper
            actt[ch, k] = act.astype(BF)
            ggt[ch, k, :H] = (err * upper * sig * (1.0 + gate * (1.0 - sig))).astype(BF)
            ggt[ch, k, H:] = (err * gate * sig).astype(BF)
            score = score + jnp.sum(err * act, axis=0, keepdims=True)
        score = jnp.broadcast_to(score, (16, 2 * rows)).astype(BF)
        mark = (iota((16, EXTRA), 0) == 0) & (iota((16, EXTRA), 1) == expert)
        value = dot(score, jnp.where(mark, 1.0, 0.0).astype(BF), 0, 0)
        rts[ch, :, :, D:] = value.astype(BF).reshape(2, rows, EXTRA)

    def rt(ch, p, to, frm):
        at, wide = pieces[ch][p]
        return remote(
            rts.at[ch, :, pl.ds(to * R, R), pl.ds(at, wide)],
            rtr.at[ch, :, pl.ds(frm * R, R), pl.ds(at, wide)],
            rt_send.at[ch, p, to],
            rt_recv.at[ch, p, frm],
            (to, e),
        )

    def rt_own(ch, p):
        at, wide = pieces[ch][p]
        return pltpu.make_async_copy(
            rts.at[ch, :, pl.ds(s * R, R), pl.ds(at, wide)],
            rtr.at[ch, :, pl.ds(s * R, R), pl.ds(at, wide)],
            rt_send.at[ch, p, s],
        )

    def compute(ch):
        forward_part(ch)
        for p, (first, width) in enumerate(pieces[ch]):
            for at, wide in tiles(min(width, D - first), 512):
                cols = slice(first + at, first + at + wide)
                w = wgu[:, :, :, cols].reshape(4 * H, wide)
                value = dot(ggt[ch].reshape(4 * H, 2 * rows), w, 0, 0)
                rts[ch, :, :, cols] = value.astype(BF).reshape(2, rows, wide)
            loop(1, G, lambda i: rt(ch, p, ahead(i), s).start())
            rt_own(ch, p).start()

    def home(ch, p):
        rt_own(ch, p).wait()

        def one(i):
            frm = behind(i)
            rt(ch, p, frm, frm).wait_recv()

        loop(1, G, one)
        first, width = pieces[ch][p]
        for at, wide in tiles(width, 512):
            cols = slice(first + at, first + at + wide)
            for j in range(2):
                n = 2 * ch + j
                value = dot(pt[n], rtr[ch, j, :, cols], 1, 0)
                tp[n * quarter : (n + 1) * quarter, :, cols] = value.reshape(quarter, B, wide)

    for i in range(2):
        wx_in(i).wait_recv()
    arrived(0)
    arrived(1)
    compute(0)
    arrived(2)
    arrived(3)
    compute(1)

    def near(i):
        return remote(nrs.at[i], nrr.at[i], nr_send.at[i], nr_recv.at[i], along(NEAR[i]))

    home(0, 0)
    for i, rel in enumerate(NEAR):
        nrs[i] = tp[POS[rel]].astype(BF)
        near(i).start()

    def weight_grads(k, put):
        for at, wide in tiles(D, 512):
            cols = slice(at, at + wide)
            total = jnp.zeros((2 * H, wide), F32)
            total_down = jnp.zeros((H, wide), F32)
            for ch in range(2):
                x = rbuf[ch, 0, :, :, cols].reshape(2 * rows, wide)
                dy = rbuf[ch, 1, :, :, cols].reshape(2 * rows, wide)
                total = total + dot(ggt[ch, k], x, 1, 0)
                total_down = total_down + dot(actt[ch, k], dy, 1, 0)
            put[: 2 * H, cols] = total
            put[2 * H :, cols] = total_down

    wg = remote(wg_snd, wg_rcv, wx_send.at[2], wx_recv.at[2], partner)
    weight_grads(1 - c, wg_snd)
    wg.start()
    weight_grads(c, wg_own)

    spans = pieces[1]

    def far(i, p):
        cols = pl.ds(*spans[p])
        return remote(
            frs.at[i, :, cols],
            frr.at[i, :, cols],
            fr_send.at[i, p],
            fr_recv.at[i, p],
            along(FAR[i][0]),
        )

    def final(i, p):
        cols = pl.ds(*spans[p])
        return remote(
            lrs.at[i, :, cols],
            lrr.at[i, :, cols],
            lr_send.at[i, p],
            lr_recv.at[i, p],
            along(LAST[i][0]),
        )

    def second_hop(p):
        cols = slice(spans[p][0], sum(spans[p]))
        for way, (_, rel) in enumerate(LAST):
            total = tp[POS[rel], :, cols]
            for i, (_, _, which) in enumerate(FAR):
                if which == way:
                    far(i, p).wait_recv()
                    total = total + frr[i, :, cols].astype(F32)
            lrs[way, :, cols] = total.astype(BF)
            final(way, p).start()

    for p in range(len(spans)):
        home(1, p)
        cols = slice(spans[p][0], sum(spans[p]))
        for i, (_, rel, _) in enumerate(FAR):
            frs[i, :, cols] = tp[POS[rel], :, cols].astype(BF)
            far(i, p).start()
        if p > 0:
            second_hop(p - 1)
    second_hop(len(spans) - 1)

    wg.wait_recv()
    for at, wide in tiles(D, 512):
        cols = slice(at, at + wide)
        total = (wg_own[:, cols] + wg_rcv[:, cols]).astype(BF)
        ggu[:, :, cols] = total[: 2 * H].reshape(2, H, wide)
        gd[:, cols] = total[2 * H :]
    o_copies = [
        pltpu.make_async_copy(ggu, ggu_hbm.at[0], o_sem.at[0]),
        pltpu.make_async_copy(gd, gd_hbm.at[0], o_sem.at[1]),
    ]
    for copy in o_copies:
        copy.start()

    for i in range(len(NEAR)):
        near(i).wait_recv()
    for p in range(len(spans)):
        first, width = spans[p]
        cols = slice(first, first + width)
        total = tp[own, :, cols]
        for i in range(len(NEAR)):
            total = total + nrr[i, :, cols].astype(F32)
        for way in range(2):
            final(way, p).wait_recv()
            total = total + lrr[way, :, cols].astype(F32)
        if first + width == W2:
            scores = total[:, width - EXTRA :]
            total = total[:, : width - EXTRA]
        gt_ref[:, first : first + total.shape[1]] = total.astype(BF)
    lanes = lane.astype(F32)
    for k in range(top):
        hit = jnp.broadcast_to(ids[:, k : k + 1], (B, EXTRA)) == lanes
        value = jnp.sum(jnp.where(hit, scores, 0.0), axis=1, keepdims=True)
        gp_ref[:, k : k + 1] = value / probs[:, k : k + 1]

    for piece in range(2):
        for way in range(2):
            for i in range(last[way] + 1):
                ag(way, i, piece).wait_send()
    for i in range(2):
        wx(i).wait_send()
    wg.wait_send()
    for n in range(4):
        for piece in range(2):
            loop(1, G, lambda i: ip(n, piece, ahead(i), s).wait_send())
    for ch in range(2):
        for p in range(len(pieces[ch])):
            loop(1, G, lambda i: rt(ch, p, ahead(i), s).wait_send())
    for i in range(len(NEAR)):
        near(i).wait_send()
    for p in range(len(spans)):
        for i in range(len(FAR)):
            far(i, p).wait_send()
        for i in range(len(LAST)):
            final(i, p).wait_send()
    for copy in o_copies:
        copy.wait()


def hand_over(*refs):
    count = (len(refs) - 2) // 3
    ins, outs, held = refs[:count], refs[count : 2 * count], refs[2 * count : 3 * count]
    in_sem, out_sem = refs[-2:]
    reads = [pltpu.make_async_copy(ins[i], held[i], in_sem.at[i]) for i in range(count)]
    writes = [pltpu.make_async_copy(held[i], outs[i], out_sem.at[i]) for i in range(count)]
    for copy in reads:
        copy.start()
    for read, write in zip(reads, writes):
        read.wait()
        write.start()
    for copy in writes:
        copy.wait()


def body(tokens, out_grads, route_ids, route_probs, w_gate_up, w_down):
    B, D = tokens.shape
    top = route_ids.shape[1]
    H = w_down.shape[1]
    G = lax.axis_size("seq")
    Z = lax.axis_size("expert") // 2
    half = Z // 2
    quarter = Z // 4
    rows = G * quarter * CAP
    nt = quarter * B
    W2 = D + EXTRA
    pieces = (((0, W2),), ((0, D // 2), (D // 2, D // 2 + EXTRA)))
    count = max(len(p) for p in pieces)
    vmem = pl.BlockSpec(memory_space=pltpu.VMEM)
    anys = pl.BlockSpec(memory_space=pl.ANY)
    dma = pltpu.SemaphoreType.DMA
    outs = (
        jax.ShapeDtypeStruct((B, D), BF),
        jax.ShapeDtypeStruct((B, top), F32),
        jax.ShapeDtypeStruct(w_gate_up.shape, BF),
        jax.ShapeDtypeStruct(w_down.shape, BF),
    )
    gt, gp, ggu, gd = pl.pallas_call(
        functools.partial(kernel, G, Z, top, pieces),
        out_shape=outs,
        in_specs=[vmem, vmem, vmem, vmem, anys, anys],
        out_specs=(vmem, vmem, anys, anys),
        scratch_shapes=[
            pltpu.VMEM((Z, B, W2), BF),
            pltpu.VMEM((Z, B, D), BF),
            pltpu.VMEM((2, 2, 2, rows, D), BF),
            pltpu.VMEM((2, 2, 2, rows, D), BF),
            pltpu.VMEM((4, nt, rows), BF),
            pltpu.VMEM((2, 2, H, D), BF),
            pltpu.VMEM((2, H, D), BF),
            pltpu.VMEM((2, 2, 2 * H, 2 * rows), BF),
            pltpu.VMEM((2, 2, H, 2 * rows), BF),
            pltpu.VMEM((2, 2, rows, W2), BF),
            pltpu.VMEM((2, 2, rows, W2), BF),
            pltpu.VMEM((Z, B, W2), F32),
            pltpu.VMEM((len(NEAR), B, W2), BF),
            pltpu.VMEM((len(NEAR), B, W2), BF),
            pltpu.VMEM((len(FAR), B, W2), BF),
            pltpu.VMEM((len(FAR), B, W2), BF),
            pltpu.VMEM((len(LAST), B, W2), BF),
            pltpu.VMEM((len(LAST), B, W2), BF),
            pltpu.VMEM((3 * H, D), F32),
            pltpu.VMEM((3 * H, D), F32),
            pltpu.VMEM((3 * H, D), F32),
            pltpu.VMEM((2, H, D), BF),
            pltpu.VMEM((H, D), BF),
            dma((2, 2, half)),
            dma((2, 2, half)),
            dma((4, 2, G)),
            dma((4, 2, G)),
            dma((2, count, G)),
            dma((2, count, G)),
            dma((len(NEAR),)),
            dma((len(NEAR),)),
            dma((len(FAR), count)),
            dma((len(FAR), count)),
            dma((len(LAST), count)),
            dma((len(LAST), count)),
            dma((3,)),
            dma((3,)),
            dma((2,)),
            dma((2,)),
        ],
        compiler_params=pltpu.CompilerParams(
            collective_id=0, has_side_effects=True, vmem_limit_bytes=56 * 1024 * 1024
        ),
        name="moe_backward",
    )(tokens, out_grads, route_ids, route_probs, w_gate_up, w_down)
    gt, ggu, gd = pl.pallas_call(
        hand_over,
        out_shape=(outs[0], outs[2], outs[3]),
        in_specs=[anys] * 3,
        out_specs=(anys,) * 3,
        scratch_shapes=[
            pltpu.VMEM(tokens.shape, BF),
            pltpu.VMEM(w_gate_up.shape, BF),
            pltpu.VMEM(w_down.shape, BF),
            dma((3,)),
            dma((3,)),
        ],
        name="hand_over",
    )(gt, ggu, gd)
    return gt, gp, ggu, gd


def solution(mesh):
    in_specs = (
        P(("seq", "expert"), None),
        P(("seq", "expert"), None),
        P(("seq", "expert"), None),
        P(("seq", "expert"), None),
        P(("seq", "expert"), None, None, None),
        P(("seq", "expert"), None, None),
    )
    out_specs = (
        P(("seq", "expert"), None),
        P(("seq", "expert"), None),
        P(("seq", "expert"), None, None, None),
        P(("seq", "expert"), None, None),
    )
    return jax.shard_map(body, mesh=mesh, in_specs=in_specs, out_specs=out_specs, check_vma=False)
```

```python
import functools

import jax
import jax.numpy as jnp
from jax import lax
from jax.experimental import pallas as pl
from jax.experimental.pallas import tpu as pltpu
from jax.sharding import PartitionSpec as P

MESH = pl.DeviceIdType.MESH
CAP = 2
EXTRA = 128
BF = jnp.bfloat16
F32 = jnp.float32


def dot(a, b, ca, cb):
    return lax.dot_general(a, b, (((ca,), (cb,)), ((), ())), preferred_element_type=F32)


def tiles(width, size):
    return [(at, min(size, width - at)) for at in range(0, width, size)]


BLOCKS = (-2, -1, 0, 1, -4, -3, 2, 3, -6, -5, 4, 5, -8, -7, 6, 7)
POS = {rel: at for at, rel in enumerate(BLOCKS)}
NEAR = (-4, 3, -3, 2, -2, 1, -1)
FAR = ((1, 6, 0), (2, 7, 0), (-1, 4, 0), (1, -5, 1), (-1, -7, 1), (-2, -8, 1))
LAST = ((5, 5), (-6, -6))
GREET = (-3, -2, -1, 1, 2, 3, 4, -5, 6)


def kernel(
    G,
    Z,
    top,
    pieces,
    tok_ref,
    og_ref,
    ids_ref,
    probs_ref,
    wgu_hbm,
    wd_hbm,
    gt_ref,
    gp_ref,
    ggu_hbm,
    gd_hbm,
    xm,
    dyb,
    sbuf,
    rbuf,
    pt,
    wgu,
    wd,
    ggt,
    actt,
    rts,
    rtr,
    tp,
    nrs,
    nrr,
    frs,
    frr,
    lrs,
    lrr,
    wg_own,
    wg_snd,
    wg_rcv,
    ggu,
    gd,
    ag_send,
    ag_recv,
    ip_send,
    ip_recv,
    rt_send,
    rt_recv,
    nr_send,
    nr_recv,
    fr_send,
    fr_recv,
    lr_send,
    lr_recv,
    wx_send,
    wx_recv,
    w_sem,
    o_sem,
):
    B, D = tok_ref.shape
    H = wd.shape[1]
    W2 = D + EXTRA
    half = Z // 2
    quarter = Z // 4
    R = quarter * CAP
    rows = G * R
    nt = quarter * B
    side = 4 if G == 16 else 0

    s = lax.axis_index("seq")
    e = lax.axis_index("expert")
    z = e // 2
    c = e % 2
    q = e // (Z * 2 // 4)
    expert = s * 4 + q
    partner = (s, z * 2 + 1 - c)

    def along(k):
        return (s, lax.rem(z + Z + k, Z) * 2 + c)

    if side:
        ys = [lax.rem(s // side + k, side) * side for k in range(side)]
        xs = [lax.rem(s % side + k, side) for k in range(side)]
        ahead = [ys[i // side] + xs[i % side] for i in range(G)]
        behind = [ys[-(i // side) % side] + xs[-(i % side) % side] for i in range(G)]
    else:
        ahead = [lax.rem(s + i, G) for i in range(G)]
        behind = [lax.rem(s + G - i, G) for i in range(G)]

    def iota(shape, dim):
        return lax.broadcasted_iota(jnp.int32, shape, dim)

    def log2(n):
        return n.bit_length() - 1

    def remote(src, dst, send, recv, to):
        return pltpu.make_async_remote_copy(
            src_ref=src,
            dst_ref=dst,
            send_sem=send,
            recv_sem=recv,
            device_id=to,
            device_id_type=MESH,
        )

    w_copies = [
        pltpu.make_async_copy(wgu_hbm.at[0], wgu.at[c], w_sem.at[0]),
        pltpu.make_async_copy(wd_hbm.at[0], wd.at[c], w_sem.at[1]),
    ]
    for copy in w_copies:
        copy.start()

    barrier = pltpu.get_barrier_semaphore()

    for i in range(1, G):
        pl.semaphore_signal(barrier, inc=1, device_id=(ahead[i], e), device_id_type=MESH)
    for k in GREET:
        pl.semaphore_signal(barrier, inc=1, device_id=along(k), device_id_type=MESH)
    pl.semaphore_signal(barrier, inc=1, device_id=partner, device_id_type=MESH)

    def placed(ref, first):
        lanes = jnp.where(iota((top, EXTRA), 1) == iota((top, EXTRA), 0) + first, 1.0, 0.0)
        return dot(ref[...].astype(BF), lanes.astype(BF), 0, 0)

    own_meta = placed(ids_ref, 0) + placed(probs_ref, 8)
    own = POS[0]
    xm[own, :, :D] = tok_ref[...]
    xm[own, :, D:] = own_meta.astype(BF)
    dyb[own] = og_ref[...]

    pl.semaphore_wait(barrier, G - 1 + len(GREET) + 1)

    def ag(way, i, piece):
        buf = xm if piece == 0 else dyb
        src, dst = (-i, -i - 1) if way == 0 else (i, i + 1)
        return remote(
            buf.at[POS[src]],
            buf.at[POS[dst]],
            ag_send.at[way, piece, i],
            ag_recv.at[way, piece, i],
            along(1 if way == 0 else -1),
        )

    last = (half - 1, half - 2)

    def ag_step(i):
        for piece in range(2):
            for way in range(2):
                if 0 <= i - 1 <= last[way]:
                    ag(way, i - 1, piece).wait_recv()
                if i <= last[way]:
                    ag(way, i, piece).start()

    def wx(i):
        src = wgu if i == 0 else wd
        return remote(src.at[c], src.at[c], wx_send.at[i], wx_recv.at[i], partner)

    def wx_in(i):
        src = wgu if i == 0 else wd
        return remote(src.at[1 - c], src.at[1 - c], wx_send.at[i], wx_recv.at[i], partner)

    def ip(n, piece, i, to, frm):
        return remote(
            sbuf.at[n // 2, piece, n % 2, pl.ds(to * R, R)],
            rbuf.at[n // 2, piece, n % 2, pl.ds(frm * R, R)],
            ip_send.at[n, piece, i],
            ip_recv.at[n, piece, i],
            (to, e),
        )

    def ip_own(n, piece):
        return pltpu.make_async_copy(
            sbuf.at[n // 2, piece, n % 2, pl.ds(s * R, R)],
            rbuf.at[n // 2, piece, n % 2, pl.ds(s * R, R)],
            ip_send.at[n, piece, 0],
        )

    def pick(n):
        blocks = pl.ds(n * quarter, quarter)
        meta = xm[blocks, :, D:].reshape(nt, EXTRA).astype(F32)
        lane_expert = (iota((nt, EXTRA), 1) * 4 + q).astype(F32)
        member = jnp.zeros((nt, EXTRA), F32)
        weight = jnp.zeros((nt, EXTRA), F32)
        for k in range(top):
            hit = jnp.broadcast_to(meta[:, k : k + 1], (nt, EXTRA)) == lane_expert
            member = member + jnp.where(hit, 1.0, 0.0)
            weight = weight + jnp.where(
                hit, jnp.broadcast_to(meta[:, 8 + k : 9 + k], (nt, EXTRA)), 0.0
            )
        member = member.astype(BF)
        weight = weight.astype(BF)
        ti, tj = iota((nt, nt), 0), iota((nt, nt), 1)
        earlier = ((ti >> log2(B)) == (tj >> log2(B))) & (tj < ti)
        rank = dot(jnp.where(earlier, 1.0, 0.0).astype(BF), member, 1, 0).astype(BF)
        spread = jnp.where(
            iota((EXTRA, rows), 0) == (iota((EXTRA, rows), 1) >> log2(R)), 1.0, 0.0
        ).astype(BF)
        member_s = dot(member, spread, 1, 0)
        rank_s = dot(rank, spread, 1, 0)
        weight_s = dot(weight, spread, 1, 0)
        tok, slot = iota((nt, rows), 0), iota((nt, rows), 1)
        mine = (tok >> log2(B)) == ((slot & (R - 1)) >> 1)
        chosen = (member_s > 0.5) & (rank_s == (slot & 1).astype(F32)) & mine
        picked = jnp.where(chosen, 1.0, 0.0).astype(BF)
        pt[n] = picked
        for piece in range(2):
            matrix = picked if piece == 0 else jnp.where(chosen, weight_s, 0.0).astype(BF)
            for at, wide in tiles(D, 512):
                if piece == 0:
                    block = xm[blocks, :, at : at + wide].reshape(nt, wide)
                else:
                    block = dyb[blocks, :, at : at + wide].reshape(nt, wide)
                value = dot(matrix, block, 0, 0).astype(BF)
                sbuf[n // 2, piece, n % 2, :, at : at + wide] = value
            for i in range(1, G):
                ip(n, piece, i, ahead[i], s).start()
            ip_own(n, piece).start()

    ag_step(0)
    for copy in w_copies:
        copy.wait()
    for i in range(2):
        wx(i).start()
    for n in range(4):
        ag_step(2 * n + 1)
        ag_step(2 * n + 2)
        pick(n)

    def arrived(n):
        for piece in range(2):
            ip_own(n, piece).wait()
            for i in range(1, G):
                ip(n, piece, i, behind[i], behind[i]).wait_recv()

    def forward_part(ch):
        x = rbuf[ch, 0].reshape(2 * rows, D)
        dy = rbuf[ch, 1].reshape(2 * rows, D)
        score = jnp.zeros((1, 2 * rows), F32)
        for k in range(2):
            gu = dot(wgu[k].reshape(2 * H, D), x, 1, 1)
            gate, upper = gu[:H], gu[H:]
            err = dot(wd[k], dy, 1, 1)
            sig = jax.nn.sigmoid(gate)
            act = gate * sig * upper
            actt[ch, k] = act.astype(BF)
            ggt[ch, k, :H] = (err * upper * sig * (1.0 + gate * (1.0 - sig))).astype(BF)
            ggt[ch, k, H:] = (err * gate * sig).astype(BF)
            score = score + jnp.sum(err * act, axis=0, keepdims=True)
        score = jnp.broadcast_to(score, (16, 2 * rows)).astype(BF)
        mark = (iota((16, EXTRA), 0) == 0) & (iota((16, EXTRA), 1) == expert)
        value = dot(score, jnp.where(mark, 1.0, 0.0).astype(BF), 0, 0)
        rts[ch, :, :, D:] = value.astype(BF).reshape(2, rows, EXTRA)

    def rt(ch, p, i, to, frm):
        at, wide = pieces[ch][p]
        return remote(
            rts.at[ch, :, pl.ds(to * R, R), pl.ds(at, wide)],
            rtr.at[ch, :, pl.ds(frm * R, R), pl.ds(at, wide)],
            rt_send.at[ch, p, i],
            rt_recv.at[ch, p, i],
            (to, e),
        )

    def rt_own(ch, p):
        at, wide = pieces[ch][p]
        return pltpu.make_async_copy(
            rts.at[ch, :, pl.ds(s * R, R), pl.ds(at, wide)],
            rtr.at[ch, :, pl.ds(s * R, R), pl.ds(at, wide)],
            rt_send.at[ch, p, 0],
        )

    def row_grads(ch, p):
        first, width = pieces[ch][p]
        for at, wide in tiles(min(width, D - first), 512):
            cols = slice(first + at, first + at + wide)
            w = wgu[:, :, :, cols].reshape(4 * H, wide)
            value = dot(ggt[ch].reshape(4 * H, 2 * rows), w, 0, 0)
            rts[ch, :, :, cols] = value.astype(BF).reshape(2, rows, wide)

    def send_back(ch, p):
        for i in range(1, G):
            rt(ch, p, i, ahead[i], s).start()
        rt_own(ch, p).start()

    def home(ch, p):
        rt_own(ch, p).wait()
        for i in range(1, G):
            rt(ch, p, i, behind[i], behind[i]).wait_recv()
        first, width = pieces[ch][p]
        for at, wide in tiles(width, 512):
            cols = slice(first + at, first + at + wide)
            for j in range(2):
                n = 2 * ch + j
                value = dot(pt[n], rtr[ch, j, :, cols], 1, 0)
                tp[n * quarter : (n + 1) * quarter, :, cols] = value.reshape(quarter, B, wide)

    for i in range(2):
        wx_in(i).wait_recv()
    arrived(0)
    arrived(1)
    forward_part(0)
    row_grads(0, 0)
    send_back(0, 0)
    arrived(2)
    arrived(3)
    forward_part(1)
    for p in range(len(pieces[1])):
        row_grads(1, p)
        send_back(1, p)

    def weight_grads(k, put):
        for at, wide in tiles(D, 512):
            cols = slice(at, at + wide)
            total = jnp.zeros((2 * H, wide), F32)
            total_down = jnp.zeros((H, wide), F32)
            for ch in range(2):
                x = rbuf[ch, 0, :, :, cols].reshape(2 * rows, wide)
                dy = rbuf[ch, 1, :, :, cols].reshape(2 * rows, wide)
                total = total + dot(ggt[ch, k], x, 1, 0)
                total_down = total_down + dot(actt[ch, k], dy, 1, 0)
            put[: 2 * H, cols] = total
            put[2 * H :, cols] = total_down

    wg = remote(wg_snd, wg_rcv, wx_send.at[2], wx_recv.at[2], partner)
    weight_grads(1 - c, wg_snd)
    wg.start()
    weight_grads(c, wg_own)

    def near(i):
        return remote(nrs.at[i], nrr.at[i], nr_send.at[i], nr_recv.at[i], along(NEAR[i]))

    home(0, 0)
    for i, rel in enumerate(NEAR):
        nrs[i] = tp[POS[rel]].astype(BF)
        near(i).start()

    spans = pieces[1]

    def far(i, p):
        cols = pl.ds(*spans[p])
        return remote(
            frs.at[i, :, cols],
            frr.at[i, :, cols],
            fr_send.at[i, p],
            fr_recv.at[i, p],
            along(FAR[i][0]),
        )

    def final(i, p):
        cols = pl.ds(*spans[p])
        return remote(
            lrs.at[i, :, cols],
            lrr.at[i, :, cols],
            lr_send.at[i, p],
            lr_recv.at[i, p],
            along(LAST[i][0]),
        )

    def second_hop(p):
        cols = slice(spans[p][0], sum(spans[p]))
        for way, (_, rel) in enumerate(LAST):
            total = tp[POS[rel], :, cols]
            for i, (_, _, which) in enumerate(FAR):
                if which == way:
                    far(i, p).wait_recv()
                    total = total + frr[i, :, cols].astype(F32)
            lrs[way, :, cols] = total.astype(BF)
            final(way, p).start()

    for p in range(len(spans)):
        home(1, p)
        cols = slice(spans[p][0], sum(spans[p]))
        for i, (_, rel, _) in enumerate(FAR):
            frs[i, :, cols] = tp[POS[rel], :, cols].astype(BF)
            far(i, p).start()
        if p > 0:
            second_hop(p - 1)
    second_hop(len(spans) - 1)

    wg.wait_recv()
    for at, wide in tiles(D, 512):
        cols = slice(at, at + wide)
        total = (wg_own[:, cols] + wg_rcv[:, cols]).astype(BF)
        ggu[:, :, cols] = total[: 2 * H].reshape(2, H, wide)
        gd[:, cols] = total[2 * H :]
    o_copies = [
        pltpu.make_async_copy(ggu, ggu_hbm.at[0], o_sem.at[0]),
        pltpu.make_async_copy(gd, gd_hbm.at[0], o_sem.at[1]),
    ]
    for copy in o_copies:
        copy.start()

    for i in range(len(NEAR)):
        near(i).wait_recv()
    for p in range(len(spans)):
        first, width = spans[p]
        cols = slice(first, first + width)
        total = tp[own, :, cols]
        for i in range(len(NEAR)):
            total = total + nrr[i, :, cols].astype(F32)
        for way in range(2):
            final(way, p).wait_recv()
            total = total + lrr[way, :, cols].astype(F32)
        if first + width == W2:
            scores = total[:, width - EXTRA :]
            total = total[:, : width - EXTRA]
        gt_ref[:, first : first + total.shape[1]] = total.astype(BF)
    lanes = iota((B, EXTRA), 1).astype(F32)
    meta = xm[own, :, D:].astype(F32)
    for k in range(top):
        hit = jnp.broadcast_to(meta[:, k : k + 1], (B, EXTRA)) == lanes
        value = jnp.sum(jnp.where(hit, scores, 0.0), axis=1, keepdims=True)
        gp_ref[:, k : k + 1] = value / meta[:, 8 + k : 9 + k]

    for piece in range(2):
        for way in range(2):
            for i in range(last[way] + 1):
                ag(way, i, piece).wait_send()
    for i in range(2):
        wx(i).wait_send()
    wg.wait_send()
    for n in range(4):
        for piece in range(2):
            for i in range(1, G):
                ip(n, piece, i, ahead[i], s).wait_send()
    for ch in range(2):
        for p in range(len(pieces[ch])):
            for i in range(1, G):
                rt(ch, p, i, ahead[i], s).wait_send()
    for i in range(len(NEAR)):
        near(i).wait_send()
    for p in range(len(spans)):
        for i in range(len(FAR)):
            far(i, p).wait_send()
        for i in range(len(LAST)):
            final(i, p).wait_send()
    for copy in o_copies:
        copy.wait()


def hand_over(*refs):
    count = (len(refs) - 2) // 3
    ins, outs, held = refs[:count], refs[count : 2 * count], refs[2 * count : 3 * count]
    in_sem, out_sem = refs[-2:]
    reads = [pltpu.make_async_copy(ins[i], held[i], in_sem.at[i]) for i in range(count)]
    writes = [pltpu.make_async_copy(held[i], outs[i], out_sem.at[i]) for i in range(count)]
    for copy in reads:
        copy.start()
    for read, write in zip(reads, writes):
        read.wait()
        write.start()
    for copy in writes:
        copy.wait()


def body(tokens, out_grads, route_ids, route_probs, w_gate_up, w_down):
    B, D = tokens.shape
    top = route_ids.shape[1]
    H = w_down.shape[1]
    G = lax.axis_size("seq")
    Z = lax.axis_size("expert") // 2
    half = Z // 2
    quarter = Z // 4
    rows = G * quarter * CAP
    nt = quarter * B
    W2 = D + EXTRA
    pieces = (((0, W2),), ((0, D // 2), (D // 2, D // 2 + EXTRA)))
    count = max(len(p) for p in pieces)
    vmem = pl.BlockSpec(memory_space=pltpu.VMEM)
    anys = pl.BlockSpec(memory_space=pl.ANY)
    dma = pltpu.SemaphoreType.DMA
    outs = (
        jax.ShapeDtypeStruct((B, D), BF),
        jax.ShapeDtypeStruct((B, top), F32),
        jax.ShapeDtypeStruct(w_gate_up.shape, BF),
        jax.ShapeDtypeStruct(w_down.shape, BF),
    )
    gt, gp, ggu, gd = pl.pallas_call(
        functools.partial(kernel, G, Z, top, pieces),
        out_shape=outs,
        in_specs=[vmem, vmem, vmem, vmem, anys, anys],
        out_specs=(vmem, vmem, anys, anys),
        scratch_shapes=[
            pltpu.VMEM((Z, B, W2), BF),
            pltpu.VMEM((Z, B, D), BF),
            pltpu.VMEM((2, 2, 2, rows, D), BF),
            pltpu.VMEM((2, 2, 2, rows, D), BF),
            pltpu.VMEM((4, nt, rows), BF),
            pltpu.VMEM((2, 2, H, D), BF),
            pltpu.VMEM((2, H, D), BF),
            pltpu.VMEM((2, 2, 2 * H, 2 * rows), BF),
            pltpu.VMEM((2, 2, H, 2 * rows), BF),
            pltpu.VMEM((2, 2, rows, W2), BF),
            pltpu.VMEM((2, 2, rows, W2), BF),
            pltpu.VMEM((Z, B, W2), F32),
            pltpu.VMEM((len(NEAR), B, W2), BF),
            pltpu.VMEM((len(NEAR), B, W2), BF),
            pltpu.VMEM((len(FAR), B, W2), BF),
            pltpu.VMEM((len(FAR), B, W2), BF),
            pltpu.VMEM((len(LAST), B, W2), BF),
            pltpu.VMEM((len(LAST), B, W2), BF),
            pltpu.VMEM((3 * H, D), F32),
            pltpu.VMEM((3 * H, D), F32),
            pltpu.VMEM((3 * H, D), F32),
            pltpu.VMEM((2, H, D), BF),
            pltpu.VMEM((H, D), BF),
            dma((2, 2, half)),
            dma((2, 2, half)),
            dma((4, 2, G)),
            dma((4, 2, G)),
            dma((2, count, G)),
            dma((2, count, G)),
            dma((len(NEAR),)),
            dma((len(NEAR),)),
            dma((len(FAR), count)),
            dma((len(FAR), count)),
            dma((len(LAST), count)),
            dma((len(LAST), count)),
            dma((3,)),
            dma((3,)),
            dma((2,)),
            dma((2,)),
        ],
        compiler_params=pltpu.CompilerParams(
            collective_id=0, has_side_effects=True, vmem_limit_bytes=56 * 1024 * 1024
        ),
        name="moe_backward",
    )(tokens, out_grads, route_ids.T, route_probs.T, w_gate_up, w_down)
    gt, ggu, gd = pl.pallas_call(
        hand_over,
        out_shape=(outs[0], outs[2], outs[3]),
        in_specs=[anys] * 3,
        out_specs=(anys,) * 3,
        scratch_shapes=[
            pltpu.VMEM(tokens.shape, BF),
            pltpu.VMEM(w_gate_up.shape, BF),
            pltpu.VMEM(w_down.shape, BF),
            dma((3,)),
            dma((3,)),
        ],
        name="hand_over",
    )(gt, ggu, gd)
    return gt, gp, ggu, gd


def solution(mesh):
    in_specs = (
        P(("seq", "expert"), None),
        P(("seq", "expert"), None),
        P(("seq", "expert"), None),
        P(("seq", "expert"), None),
        P(("seq", "expert"), None, None, None),
        P(("seq", "expert"), None, None),
    )
    out_specs = (
        P(("seq", "expert"), None),
        P(("seq", "expert"), None),
        P(("seq", "expert"), None, None, None),
        P(("seq", "expert"), None, None),
    )
    return jax.shard_map(body, mesh=mesh, in_specs=in_specs, out_specs=out_specs, check_vma=False)
```

```python
import functools

import jax
import jax.numpy as jnp
from jax import lax
from jax.experimental import pallas as pl
from jax.experimental.pallas import tpu as pltpu
from jax.sharding import PartitionSpec as P

MESH = pl.DeviceIdType.MESH
CAP = 2
EXTRA = 128
BF = jnp.bfloat16
F32 = jnp.float32


def dot(a, b, ca, cb):
    return lax.dot_general(a, b, (((ca,), (cb,)), ((), ())), preferred_element_type=F32)


def tiles(width, size):
    return [(at, min(size, width - at)) for at in range(0, width, size)]


BLOCKS = (-2, -1, 0, 1, -4, -3, 2, 3, -6, -5, 4, 5, -8, -7, 6, 7)
POS = {rel: at for at, rel in enumerate(BLOCKS)}
NEAR = (-4, 3, -3, 2, -2, 1, -1)
FAR = ((1, 6, 0), (2, 7, 0), (-1, 4, 0), (1, -5, 1), (-1, -7, 1), (-2, -8, 1))
LAST = ((5, 5), (-6, -6))
GREET = (-3, -2, -1, 1, 2, 3, 4, -5, 6)


def kernel(
    G,
    Z,
    top,
    pieces,
    tok_ref,
    og_ref,
    ids_ref,
    probs_ref,
    wgu_hbm,
    wd_hbm,
    gt_ref,
    gp_ref,
    ggu_hbm,
    gd_hbm,
    xm,
    dyb,
    sbuf,
    rbuf,
    pt,
    wgu,
    wd,
    ggt,
    actt,
    rts,
    rtr,
    tp,
    nrs,
    nrr,
    frs,
    frr,
    lrs,
    lrr,
    wg_own,
    wg_snd,
    wg_rcv,
    ggu,
    gd,
    ag_send,
    ag_recv,
    ip_send,
    ip_recv,
    rt_send,
    rt_recv,
    nr_send,
    nr_recv,
    fr_send,
    fr_recv,
    lr_send,
    lr_recv,
    wx_send,
    wx_recv,
    w_sem,
    o_sem,
):
    B, D = tok_ref.shape
    H = wd.shape[1]
    W2 = D + EXTRA
    half = Z // 2
    quarter = Z // 4
    R = quarter * CAP
    rows = G * R
    nt = quarter * B
    side = 4 if G == 16 else 0

    s = lax.axis_index("seq")
    e = lax.axis_index("expert")
    z = e // 2
    c = e % 2
    q = e // (Z * 2 // 4)
    expert = s * 4 + q
    partner = (s, z * 2 + 1 - c)

    def along(k):
        return (s, lax.rem(z + Z + k, Z) * 2 + c)

    if side:
        ys = [lax.rem(s // side + k, side) * side for k in range(side)]
        xs = [lax.rem(s % side + k, side) for k in range(side)]
        ahead = [ys[i // side] + xs[i % side] for i in range(G)]
        behind = [ys[-(i // side) % side] + xs[-(i % side) % side] for i in range(G)]
    else:
        ahead = [lax.rem(s + i, G) for i in range(G)]
        behind = [lax.rem(s + G - i, G) for i in range(G)]

    def iota(shape, dim):
        return lax.broadcasted_iota(jnp.int32, shape, dim)

    def log2(n):
        return n.bit_length() - 1

    def remote(src, dst, send, recv, to):
        return pltpu.make_async_remote_copy(
            src_ref=src,
            dst_ref=dst,
            send_sem=send,
            recv_sem=recv,
            device_id=to,
            device_id_type=MESH,
        )

    w_copies = [
        pltpu.make_async_copy(wgu_hbm.at[0], wgu.at[c], w_sem.at[0]),
        pltpu.make_async_copy(wd_hbm.at[0], wd.at[c], w_sem.at[1]),
    ]
    for copy in w_copies:
        copy.start()

    barrier = pltpu.get_barrier_semaphore()

    for i in range(1, G):
        pl.semaphore_signal(barrier, inc=1, device_id=(ahead[i], e), device_id_type=MESH)
    for k in GREET:
        pl.semaphore_signal(barrier, inc=1, device_id=along(k), device_id_type=MESH)
    pl.semaphore_signal(barrier, inc=1, device_id=partner, device_id_type=MESH)

    def placed(ref, first):
        lanes = jnp.where(iota((top, EXTRA), 1) == iota((top, EXTRA), 0) + first, 1.0, 0.0)
        return dot(ref[...].astype(BF), lanes.astype(BF), 0, 0)

    own_meta = placed(ids_ref, 0) + placed(probs_ref, 8)
    own = POS[0]
    xm[own, :, :D] = tok_ref[...]
    xm[own, :, D:] = own_meta.astype(BF)
    dyb[own] = og_ref[...]

    pl.semaphore_wait(barrier, G - 1 + len(GREET) + 1)

    def ag(way, i, piece):
        buf = xm if piece == 0 else dyb
        src, dst = (-i, -i - 1) if way == 0 else (i, i + 1)
        return remote(
            buf.at[POS[src]],
            buf.at[POS[dst]],
            ag_send.at[way, piece, i],
            ag_recv.at[way, piece, i],
            along(1 if way == 0 else -1),
        )

    last = (half - 1, half - 2)

    def ag_step(i):
        for piece in range(2):
            for way in range(2):
                if 0 <= i - 1 <= last[way]:
                    ag(way, i - 1, piece).wait_recv()
                if i <= last[way]:
                    ag(way, i, piece).start()

    def wx(i):
        src = wgu if i == 0 else wd
        return remote(src.at[c], src.at[c], wx_send.at[i], wx_recv.at[i], partner)

    def wx_in(i):
        src = wgu if i == 0 else wd
        return remote(src.at[1 - c], src.at[1 - c], wx_send.at[i], wx_recv.at[i], partner)

    def ip(n, piece, i, to, frm):
        return remote(
            sbuf.at[n // 2, piece, n % 2, pl.ds(to * R, R)],
            rbuf.at[n // 2, piece, n % 2, pl.ds(frm * R, R)],
            ip_send.at[n, piece, i],
            ip_recv.at[n, piece, i],
            (to, e),
        )

    def ip_own(n, piece):
        return pltpu.make_async_copy(
            sbuf.at[n // 2, piece, n % 2, pl.ds(s * R, R)],
            rbuf.at[n // 2, piece, n % 2, pl.ds(s * R, R)],
            ip_send.at[n, piece, 0],
        )

    def pick(n):
        blocks = pl.ds(n * quarter, quarter)
        meta = xm[blocks, :, D:].reshape(nt, EXTRA).astype(F32)
        lane_expert = (iota((nt, EXTRA), 1) * 4 + q).astype(F32)
        member = jnp.zeros((nt, EXTRA), F32)
        weight = jnp.zeros((nt, EXTRA), F32)
        for k in range(top):
            hit = jnp.broadcast_to(meta[:, k : k + 1], (nt, EXTRA)) == lane_expert
            member = member + jnp.where(hit, 1.0, 0.0)
            weight = weight + jnp.where(
                hit, jnp.broadcast_to(meta[:, 8 + k : 9 + k], (nt, EXTRA)), 0.0
            )
        member = member.astype(BF)
        weight = weight.astype(BF)
        ti, tj = iota((nt, nt), 0), iota((nt, nt), 1)
        earlier = ((ti >> log2(B)) == (tj >> log2(B))) & (tj < ti)
        rank = dot(jnp.where(earlier, 1.0, 0.0).astype(BF), member, 1, 0).astype(BF)
        spread = jnp.where(
            iota((EXTRA, rows), 0) == (iota((EXTRA, rows), 1) >> log2(R)), 1.0, 0.0
        ).astype(BF)
        member_s = dot(member, spread, 1, 0)
        rank_s = dot(rank, spread, 1, 0)
        weight_s = dot(weight, spread, 1, 0)
        tok, slot = iota((nt, rows), 0), iota((nt, rows), 1)
        mine = (tok >> log2(B)) == ((slot & (R - 1)) >> 1)
        chosen = (member_s > 0.5) & (rank_s == (slot & 1).astype(F32)) & mine
        picked = jnp.where(chosen, 1.0, 0.0).astype(BF)
        pt[n] = picked
        for piece in range(2):
            matrix = picked if piece == 0 else jnp.where(chosen, weight_s, 0.0).astype(BF)
            for at, wide in tiles(D, 512):
                if piece == 0:
                    block = xm[blocks, :, at : at + wide].reshape(nt, wide)
                else:
                    block = dyb[blocks, :, at : at + wide].reshape(nt, wide)
                value = dot(matrix, block, 0, 0).astype(BF)
                sbuf[n // 2, piece, n % 2, :, at : at + wide] = value
            for i in range(1, G):
                ip(n, piece, i, ahead[i], s).start()
            ip_own(n, piece).start()

    ag_step(0)
    for copy in w_copies:
        copy.wait()
    for i in range(2):
        wx(i).start()
    for n in range(4):
        ag_step(2 * n + 1)
        ag_step(2 * n + 2)
        pick(n)

    def arrived(n):
        for piece in range(2):
            ip_own(n, piece).wait()
            for i in range(1, G):
                ip(n, piece, i, behind[i], behind[i]).wait_recv()

    def forward_part(ch):
        x = rbuf[ch, 0].reshape(2 * rows, D)
        dy = rbuf[ch, 1].reshape(2 * rows, D)
        score = jnp.zeros((1, 2 * rows), F32)
        for k in range(2):
            gu = dot(wgu[k].reshape(2 * H, D), x, 1, 1)
            gate, upper = gu[:H], gu[H:]
            err = dot(wd[k], dy, 1, 1)
            sig = jax.nn.sigmoid(gate)
            act = gate * sig * upper
            actt[ch, k] = act.astype(BF)
            ggt[ch, k, :H] = (err * upper * sig * (1.0 + gate * (1.0 - sig))).astype(BF)
            ggt[ch, k, H:] = (err * gate * sig).astype(BF)
            score = score + jnp.sum(err * act, axis=0, keepdims=True)
        score = jnp.broadcast_to(score, (16, 2 * rows)).astype(BF)
        mark = (iota((16, EXTRA), 0) == 0) & (iota((16, EXTRA), 1) == expert)
        value = dot(score, jnp.where(mark, 1.0, 0.0).astype(BF), 0, 0)
        rts[ch, :, :, D:] = value.astype(BF).reshape(2, rows, EXTRA)

    def rt(ch, p, i, to, frm):
        at, wide = pieces[ch][p]
        return remote(
            rts.at[ch, :, pl.ds(to * R, R), pl.ds(at, wide)],
            rtr.at[ch, :, pl.ds(frm * R, R), pl.ds(at, wide)],
            rt_send.at[ch, p, i],
            rt_recv.at[ch, p, i],
            (to, e),
        )

    def rt_own(ch, p):
        at, wide = pieces[ch][p]
        return pltpu.make_async_copy(
            rts.at[ch, :, pl.ds(s * R, R), pl.ds(at, wide)],
            rtr.at[ch, :, pl.ds(s * R, R), pl.ds(at, wide)],
            rt_send.at[ch, p, 0],
        )

    def row_grads(ch, p):
        first, width = pieces[ch][p]
        for at, wide in tiles(min(width, D - first), 512):
            cols = slice(first + at, first + at + wide)
            w = wgu[:, :, :, cols].reshape(4 * H, wide)
            value = dot(ggt[ch].reshape(4 * H, 2 * rows), w, 0, 0)
            rts[ch, :, :, cols] = value.astype(BF).reshape(2, rows, wide)

    def send_back(ch, p):
        for i in range(1, G):
            rt(ch, p, i, ahead[i], s).start()
        rt_own(ch, p).start()

    def home(ch, p):
        rt_own(ch, p).wait()
        for i in range(1, G):
            rt(ch, p, i, behind[i], behind[i]).wait_recv()
        first, width = pieces[ch][p]
        for at, wide in tiles(width, 512):
            cols = slice(first + at, first + at + wide)
            for j in range(2):
                n = 2 * ch + j
                value = dot(pt[n], rtr[ch, j, :, cols], 1, 0)
                tp[n * quarter : (n + 1) * quarter, :, cols] = value.reshape(quarter, B, wide)

    for i in range(2):
        wx_in(i).wait_recv()
    arrived(0)
    arrived(1)
    forward_part(0)
    row_grads(0, 0)
    send_back(0, 0)
    row_grads(0, 1)
    arrived(2)
    arrived(3)
    forward_part(1)
    for p in range(2):
        row_grads(1, p)
        send_back(1, p)
    send_back(0, 1)

    def weight_grads(k, put):
        for at, wide in tiles(D, 512):
            cols = slice(at, at + wide)
            total = jnp.zeros((2 * H, wide), F32)
            total_down = jnp.zeros((H, wide), F32)
            for ch in range(2):
                x = rbuf[ch, 0, :, :, cols].reshape(2 * rows, wide)
                dy = rbuf[ch, 1, :, :, cols].reshape(2 * rows, wide)
                total = total + dot(ggt[ch, k], x, 1, 0)
                total_down = total_down + dot(actt[ch, k], dy, 1, 0)
            put[: 2 * H, cols] = total
            put[2 * H :, cols] = total_down

    wg = remote(wg_snd, wg_rcv, wx_send.at[2], wx_recv.at[2], partner)
    weight_grads(1 - c, wg_snd)
    wg.start()
    weight_grads(c, wg_own)

    spans = pieces[1]

    def near(i, p):
        cols = pl.ds(*spans[p])
        return remote(
            nrs.at[i, :, cols],
            nrr.at[i, :, cols],
            nr_send.at[i, p],
            nr_recv.at[i, p],
            along(NEAR[i]),
        )

    def near_out(p):
        home(0, p)
        cols = slice(spans[p][0], sum(spans[p]))
        for i, rel in enumerate(NEAR):
            nrs[i, :, cols] = tp[POS[rel], :, cols].astype(BF)
            near(i, p).start()

    def far(i, p):
        cols = pl.ds(*spans[p])
        return remote(
            frs.at[i, :, cols],
            frr.at[i, :, cols],
            fr_send.at[i, p],
            fr_recv.at[i, p],
            along(FAR[i][0]),
        )

    def final(i, p):
        cols = pl.ds(*spans[p])
        return remote(
            lrs.at[i, :, cols],
            lrr.at[i, :, cols],
            lr_send.at[i, p],
            lr_recv.at[i, p],
            along(LAST[i][0]),
        )

    def second_hop(p):
        cols = slice(spans[p][0], sum(spans[p]))
        for way, (_, rel) in enumerate(LAST):
            total = tp[POS[rel], :, cols]
            for i, (_, _, which) in enumerate(FAR):
                if which == way:
                    far(i, p).wait_recv()
                    total = total + frr[i, :, cols].astype(F32)
            lrs[way, :, cols] = total.astype(BF)
            final(way, p).start()

    def far_out(p):
        home(1, p)
        cols = slice(spans[p][0], sum(spans[p]))
        for i, (_, rel, _) in enumerate(FAR):
            frs[i, :, cols] = tp[POS[rel], :, cols].astype(BF)
            far(i, p).start()

    near_out(0)
    far_out(0)
    far_out(1)
    second_hop(0)
    second_hop(1)
    near_out(1)

    wg.wait_recv()
    for at, wide in tiles(D, 512):
        cols = slice(at, at + wide)
        total = (wg_own[:, cols] + wg_rcv[:, cols]).astype(BF)
        ggu[:, :, cols] = total[: 2 * H].reshape(2, H, wide)
        gd[:, cols] = total[2 * H :]
    o_copies = [
        pltpu.make_async_copy(ggu, ggu_hbm.at[0], o_sem.at[0]),
        pltpu.make_async_copy(gd, gd_hbm.at[0], o_sem.at[1]),
    ]
    for copy in o_copies:
        copy.start()

    for p in range(len(spans)):
        first, width = spans[p]
        cols = slice(first, first + width)
        total = tp[own, :, cols]
        for way in range(2):
            final(way, p).wait_recv()
            total = total + lrr[way, :, cols].astype(F32)
        for i in range(len(NEAR)):
            near(i, p).wait_recv()
            total = total + nrr[i, :, cols].astype(F32)
        if first + width == W2:
            scores = total[:, width - EXTRA :]
            total = total[:, : width - EXTRA]
        gt_ref[:, first : first + total.shape[1]] = total.astype(BF)
    lanes = iota((B, EXTRA), 1).astype(F32)
    meta = xm[own, :, D:].astype(F32)
    for k in range(top):
        hit = jnp.broadcast_to(meta[:, k : k + 1], (B, EXTRA)) == lanes
        value = jnp.sum(jnp.where(hit, scores, 0.0), axis=1, keepdims=True)
        gp_ref[:, k : k + 1] = value / meta[:, 8 + k : 9 + k]

    for piece in range(2):
        for way in range(2):
            for i in range(last[way] + 1):
                ag(way, i, piece).wait_send()
    for i in range(2):
        wx(i).wait_send()
    wg.wait_send()
    for n in range(4):
        for piece in range(2):
            for i in range(1, G):
                ip(n, piece, i, ahead[i], s).wait_send()
    for ch in range(2):
        for p in range(len(pieces[ch])):
            for i in range(1, G):
                rt(ch, p, i, ahead[i], s).wait_send()
    for p in range(len(spans)):
        for i in range(len(NEAR)):
            near(i, p).wait_send()
        for i in range(len(FAR)):
            far(i, p).wait_send()
        for i in range(len(LAST)):
            final(i, p).wait_send()
    for copy in o_copies:
        copy.wait()


def hand_over(*refs):
    count = (len(refs) - 2) // 3
    ins, outs, held = refs[:count], refs[count : 2 * count], refs[2 * count : 3 * count]
    in_sem, out_sem = refs[-2:]
    reads = [pltpu.make_async_copy(ins[i], held[i], in_sem.at[i]) for i in range(count)]
    writes = [pltpu.make_async_copy(held[i], outs[i], out_sem.at[i]) for i in range(count)]
    for copy in reads:
        copy.start()
    for read, write in zip(reads, writes):
        read.wait()
        write.start()
    for copy in writes:
        copy.wait()


def body(tokens, out_grads, route_ids, route_probs, w_gate_up, w_down):
    B, D = tokens.shape
    top = route_ids.shape[1]
    H = w_down.shape[1]
    G = lax.axis_size("seq")
    Z = lax.axis_size("expert") // 2
    half = Z // 2
    quarter = Z // 4
    rows = G * quarter * CAP
    nt = quarter * B
    W2 = D + EXTRA
    pieces = (((0, D // 2), (D // 2, D // 2 + EXTRA)),) * 2
    count = max(len(p) for p in pieces)
    vmem = pl.BlockSpec(memory_space=pltpu.VMEM)
    anys = pl.BlockSpec(memory_space=pl.ANY)
    dma = pltpu.SemaphoreType.DMA
    outs = (
        jax.ShapeDtypeStruct((B, D), BF),
        jax.ShapeDtypeStruct((B, top), F32),
        jax.ShapeDtypeStruct(w_gate_up.shape, BF),
        jax.ShapeDtypeStruct(w_down.shape, BF),
    )
    gt, gp, ggu, gd = pl.pallas_call(
        functools.partial(kernel, G, Z, top, pieces),
        out_shape=outs,
        in_specs=[vmem, vmem, vmem, vmem, anys, anys],
        out_specs=(vmem, vmem, anys, anys),
        scratch_shapes=[
            pltpu.VMEM((Z, B, W2), BF),
            pltpu.VMEM((Z, B, D), BF),
            pltpu.VMEM((2, 2, 2, rows, D), BF),
            pltpu.VMEM((2, 2, 2, rows, D), BF),
            pltpu.VMEM((4, nt, rows), BF),
            pltpu.VMEM((2, 2, H, D), BF),
            pltpu.VMEM((2, H, D), BF),
            pltpu.VMEM((2, 2, 2 * H, 2 * rows), BF),
            pltpu.VMEM((2, 2, H, 2 * rows), BF),
            pltpu.VMEM((2, 2, rows, W2), BF),
            pltpu.VMEM((2, 2, rows, W2), BF),
            pltpu.VMEM((Z, B, W2), F32),
            pltpu.VMEM((len(NEAR), B, W2), BF),
            pltpu.VMEM((len(NEAR), B, W2), BF),
            pltpu.VMEM((len(FAR), B, W2), BF),
            pltpu.VMEM((len(FAR), B, W2), BF),
            pltpu.VMEM((len(LAST), B, W2), BF),
            pltpu.VMEM((len(LAST), B, W2), BF),
            pltpu.VMEM((3 * H, D), F32),
            pltpu.VMEM((3 * H, D), F32),
            pltpu.VMEM((3 * H, D), F32),
            pltpu.VMEM((2, H, D), BF),
            pltpu.VMEM((H, D), BF),
            dma((2, 2, half)),
            dma((2, 2, half)),
            dma((4, 2, G)),
            dma((4, 2, G)),
            dma((2, count, G)),
            dma((2, count, G)),
            dma((len(NEAR), count)),
            dma((len(NEAR), count)),
            dma((len(FAR), count)),
            dma((len(FAR), count)),
            dma((len(LAST), count)),
            dma((len(LAST), count)),
            dma((3,)),
            dma((3,)),
            dma((2,)),
            dma((2,)),
        ],
        compiler_params=pltpu.CompilerParams(
            collective_id=0, has_side_effects=True, vmem_limit_bytes=56 * 1024 * 1024
        ),
        name="moe_backward",
    )(tokens, out_grads, route_ids.T, route_probs.T, w_gate_up, w_down)
    gt, ggu, gd = pl.pallas_call(
        hand_over,
        out_shape=(outs[0], outs[2], outs[3]),
        in_specs=[anys] * 3,
        out_specs=(anys,) * 3,
        scratch_shapes=[
            pltpu.VMEM(tokens.shape, BF),
            pltpu.VMEM(w_gate_up.shape, BF),
            pltpu.VMEM(w_down.shape, BF),
            dma((3,)),
            dma((3,)),
        ],
        name="hand_over",
    )(gt, ggu, gd)
    return gt, gp, ggu, gd


def solution(mesh):
    in_specs = (
        P(("seq", "expert"), None),
        P(("seq", "expert"), None),
        P(("seq", "expert"), None),
        P(("seq", "expert"), None),
        P(("seq", "expert"), None, None, None),
        P(("seq", "expert"), None, None),
    )
    out_specs = (
        P(("seq", "expert"), None),
        P(("seq", "expert"), None),
        P(("seq", "expert"), None, None, None),
        P(("seq", "expert"), None, None),
    )
    return jax.shard_map(body, mesh=mesh, in_specs=in_specs, out_specs=out_specs, check_vma=False)
```

```python
import functools

import jax
import jax.numpy as jnp
from jax import lax
from jax.experimental import pallas as pl
from jax.experimental.pallas import tpu as pltpu
from jax.sharding import PartitionSpec as P

MESH = pl.DeviceIdType.MESH
CAP = 2
EXTRA = 128
BF = jnp.bfloat16
F32 = jnp.float32


def dot(a, b, ca, cb):
    return lax.dot_general(a, b, (((ca,), (cb,)), ((), ())), preferred_element_type=F32)


def tiles(width, size):
    return [(at, min(size, width - at)) for at in range(0, width, size)]


BLOCKS = (-2, -1, 0, 1, -4, -3, 2, 3, -6, -5, 4, 5, -8, -7, 6, 7)
POS = {rel: at for at, rel in enumerate(BLOCKS)}
NEAR = (-4, 3, -3, 2, -2, 1, -1)
FAR = ((1, 6, 0), (2, 7, 0), (-1, 4, 0), (1, -5, 1), (-1, -7, 1), (-2, -8, 1))
LAST = ((5, 5), (-6, -6))
GREET = (-3, -2, -1, 1, 2, 3, 4, -5, 6)


def kernel(
    G,
    Z,
    top,
    pieces,
    tok_ref,
    og_ref,
    ids_ref,
    probs_ref,
    wgu_hbm,
    wd_hbm,
    gt_ref,
    gp_ref,
    ggu_ref,
    gd_ref,
    xm,
    dyb,
    sbuf,
    rbuf,
    pt,
    wgu,
    wd,
    ggt,
    actt,
    rts,
    rtr,
    tp,
    nrs,
    nrr,
    frs,
    frr,
    lrs,
    lrr,
    wg_own,
    wg_snd,
    wg_rcv,
    ag_send,
    ag_recv,
    ip_send,
    ip_recv,
    rt_send,
    rt_recv,
    nr_send,
    nr_recv,
    fr_send,
    fr_recv,
    lr_send,
    lr_recv,
    wx_send,
    wx_recv,
    w_sem,
):
    B, D = tok_ref.shape
    H = wd.shape[1]
    W2 = D + EXTRA
    half = Z // 2
    quarter = Z // 4
    R = quarter * CAP
    rows = G * R
    nt = quarter * B
    side = 4 if G == 16 else 0

    s = lax.axis_index("seq")
    e = lax.axis_index("expert")
    z = e // 2
    c = e % 2
    q = e // (Z * 2 // 4)
    expert = s * 4 + q
    partner = (s, z * 2 + 1 - c)

    def along(k):
        return (s, lax.rem(z + Z + k, Z) * 2 + c)

    if side:
        ys = [lax.rem(s // side + k, side) * side for k in range(side)]
        xs = [lax.rem(s % side + k, side) for k in range(side)]
        ahead = [ys[i // side] + xs[i % side] for i in range(G)]
        behind = [ys[-(i // side) % side] + xs[-(i % side) % side] for i in range(G)]
    else:
        ahead = [lax.rem(s + i, G) for i in range(G)]
        behind = [lax.rem(s + G - i, G) for i in range(G)]

    def iota(shape, dim):
        return lax.broadcasted_iota(jnp.int32, shape, dim)

    def log2(n):
        return n.bit_length() - 1

    def remote(src, dst, send, recv, to):
        return pltpu.make_async_remote_copy(
            src_ref=src,
            dst_ref=dst,
            send_sem=send,
            recv_sem=recv,
            device_id=to,
            device_id_type=MESH,
        )

    w_copies = [
        pltpu.make_async_copy(wgu_hbm.at[0], wgu.at[c], w_sem.at[0]),
        pltpu.make_async_copy(wd_hbm.at[0], wd.at[c], w_sem.at[1]),
    ]
    for copy in w_copies:
        copy.start()

    barrier = pltpu.get_barrier_semaphore()

    for i in range(1, G):
        pl.semaphore_signal(barrier, inc=1, device_id=(ahead[i], e), device_id_type=MESH)
    for k in GREET:
        pl.semaphore_signal(barrier, inc=1, device_id=along(k), device_id_type=MESH)
    pl.semaphore_signal(barrier, inc=1, device_id=partner, device_id_type=MESH)

    def placed(ref, first):
        lanes = jnp.where(iota((top, EXTRA), 1) == iota((top, EXTRA), 0) + first, 1.0, 0.0)
        return dot(ref[...].astype(BF), lanes.astype(BF), 0, 0)

    own_meta = placed(ids_ref, 0) + placed(probs_ref, 8)
    own = POS[0]
    xm[own, :, :D] = tok_ref[...]
    xm[own, :, D:] = own_meta.astype(BF)
    dyb[own] = og_ref[...]

    pl.semaphore_wait(barrier, G - 1 + len(GREET) + 1)

    def ag(way, i, piece):
        buf = xm if piece == 0 else dyb
        src, dst = (-i, -i - 1) if way == 0 else (i, i + 1)
        return remote(
            buf.at[POS[src]],
            buf.at[POS[dst]],
            ag_send.at[way, piece, i],
            ag_recv.at[way, piece, i],
            along(1 if way == 0 else -1),
        )

    last = (half - 1, half - 2)

    def ag_step(i):
        for piece in range(2):
            for way in range(2):
                if 0 <= i - 1 <= last[way]:
                    ag(way, i - 1, piece).wait_recv()
                if i <= last[way]:
                    ag(way, i, piece).start()

    def wx(i):
        src = wgu if i == 0 else wd
        return remote(src.at[c], src.at[c], wx_send.at[i], wx_recv.at[i], partner)

    def wx_in(i):
        src = wgu if i == 0 else wd
        return remote(src.at[1 - c], src.at[1 - c], wx_send.at[i], wx_recv.at[i], partner)

    def ip(n, piece, i, to, frm):
        return remote(
            sbuf.at[n // 2, piece, n % 2, pl.ds(to * R, R)],
            rbuf.at[n // 2, piece, n % 2, pl.ds(frm * R, R)],
            ip_send.at[n, piece, i],
            ip_recv.at[n, piece, i],
            (to, e),
        )

    def ip_own(n, piece):
        return pltpu.make_async_copy(
            sbuf.at[n // 2, piece, n % 2, pl.ds(s * R, R)],
            rbuf.at[n // 2, piece, n % 2, pl.ds(s * R, R)],
            ip_send.at[n, piece, 0],
        )

    def pick(n):
        blocks = pl.ds(n * quarter, quarter)
        meta = xm[blocks, :, D:].reshape(nt, EXTRA).astype(F32)
        lane_expert = (iota((nt, EXTRA), 1) * 4 + q).astype(F32)
        member = jnp.zeros((nt, EXTRA), F32)
        weight = jnp.zeros((nt, EXTRA), F32)
        for k in range(top):
            hit = jnp.broadcast_to(meta[:, k : k + 1], (nt, EXTRA)) == lane_expert
            member = member + jnp.where(hit, 1.0, 0.0)
            weight = weight + jnp.where(
                hit, jnp.broadcast_to(meta[:, 8 + k : 9 + k], (nt, EXTRA)), 0.0
            )
        member = member.astype(BF)
        weight = weight.astype(BF)
        ti, tj = iota((nt, nt), 0), iota((nt, nt), 1)
        earlier = ((ti >> log2(B)) == (tj >> log2(B))) & (tj < ti)
        rank = dot(jnp.where(earlier, 1.0, 0.0).astype(BF), member, 1, 0).astype(BF)
        spread = jnp.where(
            iota((EXTRA, rows), 0) == (iota((EXTRA, rows), 1) >> log2(R)), 1.0, 0.0
        ).astype(BF)
        member_s = dot(member, spread, 1, 0)
        rank_s = dot(rank, spread, 1, 0)
        weight_s = dot(weight, spread, 1, 0)
        tok, slot = iota((nt, rows), 0), iota((nt, rows), 1)
        mine = (tok >> log2(B)) == ((slot & (R - 1)) >> 1)
        chosen = (member_s > 0.5) & (rank_s == (slot & 1).astype(F32)) & mine
        picked = jnp.where(chosen, 1.0, 0.0).astype(BF)
        pt[n] = picked
        for piece in range(2):
            matrix = picked if piece == 0 else jnp.where(chosen, weight_s, 0.0).astype(BF)
            for at, wide in tiles(D, 512):
                if piece == 0:
                    block = xm[blocks, :, at : at + wide].reshape(nt, wide)
                else:
                    block = dyb[blocks, :, at : at + wide].reshape(nt, wide)
                value = dot(matrix, block, 0, 0).astype(BF)
                sbuf[n // 2, piece, n % 2, :, at : at + wide] = value
            for i in range(1, G):
                ip(n, piece, i, ahead[i], s).start()
            ip_own(n, piece).start()

    ag_step(0)
    for copy in w_copies:
        copy.wait()
    for i in range(2):
        wx(i).start()
    for n in range(4):
        ag_step(2 * n + 1)
        ag_step(2 * n + 2)
        pick(n)

    def arrived(n):
        for piece in range(2):
            ip_own(n, piece).wait()
            for i in range(1, G):
                ip(n, piece, i, behind[i], behind[i]).wait_recv()

    def forward_part(ch):
        x = rbuf[ch, 0].reshape(2 * rows, D)
        dy = rbuf[ch, 1].reshape(2 * rows, D)
        score = jnp.zeros((1, 2 * rows), F32)
        for k in range(2):
            gu = dot(wgu[k].reshape(2 * H, D), x, 1, 1)
            gate, upper = gu[:H], gu[H:]
            err = dot(wd[k], dy, 1, 1)
            sig = jax.nn.sigmoid(gate)
            act = gate * sig * upper
            actt[ch, k] = act.astype(BF)
            ggt[ch, k, :H] = (err * upper * sig * (1.0 + gate * (1.0 - sig))).astype(BF)
            ggt[ch, k, H:] = (err * gate * sig).astype(BF)
            score = score + jnp.sum(err * act, axis=0, keepdims=True)
        score = jnp.broadcast_to(score, (16, 2 * rows)).astype(BF)
        mark = (iota((16, EXTRA), 0) == 0) & (iota((16, EXTRA), 1) == expert)
        value = dot(score, jnp.where(mark, 1.0, 0.0).astype(BF), 0, 0)
        rts[ch, :, :, D:] = value.astype(BF).reshape(2, rows, EXTRA)

    def rt(ch, p, i, to, frm):
        at, wide = pieces[ch][p]
        return remote(
            rts.at[ch, :, pl.ds(to * R, R), pl.ds(at, wide)],
            rtr.at[ch, :, pl.ds(frm * R, R), pl.ds(at, wide)],
            rt_send.at[ch, p, i],
            rt_recv.at[ch, p, i],
            (to, e),
        )

    def rt_own(ch, p):
        at, wide = pieces[ch][p]
        return pltpu.make_async_copy(
            rts.at[ch, :, pl.ds(s * R, R), pl.ds(at, wide)],
            rtr.at[ch, :, pl.ds(s * R, R), pl.ds(at, wide)],
            rt_send.at[ch, p, 0],
        )

    def row_grads(ch, p):
        first, width = pieces[ch][p]
        for at, wide in tiles(min(width, D - first), 512):
            cols = slice(first + at, first + at + wide)
            w = wgu[:, :, :, cols].reshape(4 * H, wide)
            value = dot(ggt[ch].reshape(4 * H, 2 * rows), w, 0, 0)
            rts[ch, :, :, cols] = value.astype(BF).reshape(2, rows, wide)

    def send_back(ch, p):
        for i in range(1, G):
            rt(ch, p, i, ahead[i], s).start()
        rt_own(ch, p).start()

    def home(ch, p):
        rt_own(ch, p).wait()
        for i in range(1, G):
            rt(ch, p, i, behind[i], behind[i]).wait_recv()
        first, width = pieces[ch][p]
        for at, wide in tiles(width, 512):
            cols = slice(first + at, first + at + wide)
            for j in range(2):
                n = 2 * ch + j
                value = dot(pt[n], rtr[ch, j, :, cols], 1, 0)
                tp[n * quarter : (n + 1) * quarter, :, cols] = value.reshape(quarter, B, wide)

    for i in range(2):
        wx_in(i).wait_recv()
    arrived(0)
    arrived(1)
    forward_part(0)
    row_grads(0, 0)
    send_back(0, 0)
    row_grads(0, 1)
    arrived(2)
    arrived(3)
    forward_part(1)
    for p in range(2):
        row_grads(1, p)
        send_back(1, p)
    send_back(0, 1)

    def weight_grads(k, put):
        for at, wide in tiles(D, 512):
            cols = slice(at, at + wide)
            total = jnp.zeros((2 * H, wide), F32)
            total_down = jnp.zeros((H, wide), F32)
            for ch in range(2):
                x = rbuf[ch, 0, :, :, cols].reshape(2 * rows, wide)
                dy = rbuf[ch, 1, :, :, cols].reshape(2 * rows, wide)
                total = total + dot(ggt[ch, k], x, 1, 0)
                total_down = total_down + dot(actt[ch, k], dy, 1, 0)
            put[: 2 * H, cols] = total
            put[2 * H :, cols] = total_down

    wg = remote(wg_snd, wg_rcv, wx_send.at[2], wx_recv.at[2], partner)
    weight_grads(1 - c, wg_snd)
    wg.start()
    weight_grads(c, wg_own)

    spans = pieces[1]

    def near(i, p):
        cols = pl.ds(*spans[p])
        return remote(
            nrs.at[i, :, cols],
            nrr.at[i, :, cols],
            nr_send.at[i, p],
            nr_recv.at[i, p],
            along(NEAR[i]),
        )

    def near_out(p):
        home(0, p)
        cols = slice(spans[p][0], sum(spans[p]))
        for i, rel in enumerate(NEAR):
            nrs[i, :, cols] = tp[POS[rel], :, cols].astype(BF)
            near(i, p).start()

    def far(i, p):
        cols = pl.ds(*spans[p])
        return remote(
            frs.at[i, :, cols],
            frr.at[i, :, cols],
            fr_send.at[i, p],
            fr_recv.at[i, p],
            along(FAR[i][0]),
        )

    def final(i, p):
        cols = pl.ds(*spans[p])
        return remote(
            lrs.at[i, :, cols],
            lrr.at[i, :, cols],
            lr_send.at[i, p],
            lr_recv.at[i, p],
            along(LAST[i][0]),
        )

    def second_hop(p):
        cols = slice(spans[p][0], sum(spans[p]))
        for way, (_, rel) in enumerate(LAST):
            total = tp[POS[rel], :, cols]
            for i, (_, _, which) in enumerate(FAR):
                if which == way:
                    far(i, p).wait_recv()
                    total = total + frr[i, :, cols].astype(F32)
            lrs[way, :, cols] = total.astype(BF)
            final(way, p).start()

    def far_out(p):
        home(1, p)
        cols = slice(spans[p][0], sum(spans[p]))
        for i, (_, rel, _) in enumerate(FAR):
            frs[i, :, cols] = tp[POS[rel], :, cols].astype(BF)
            far(i, p).start()

    near_out(0)
    far_out(0)
    far_out(1)
    second_hop(0)
    second_hop(1)
    near_out(1)

    wg.wait_recv()
    for at, wide in tiles(D, 512):
        cols = slice(at, at + wide)
        total = (wg_own[:, cols] + wg_rcv[:, cols]).astype(BF)
        ggu_ref[0, :, :, cols] = total[: 2 * H].reshape(2, H, wide)
        gd_ref[0, :, cols] = total[2 * H :]
    for p in range(len(spans)):
        first, width = spans[p]
        cols = slice(first, first + width)
        total = tp[own, :, cols]
        for way in range(2):
            final(way, p).wait_recv()
            total = total + lrr[way, :, cols].astype(F32)
        for i in range(len(NEAR)):
            near(i, p).wait_recv()
            total = total + nrr[i, :, cols].astype(F32)
        if first + width == W2:
            scores = total[:, width - EXTRA :]
            total = total[:, : width - EXTRA]
        gt_ref[:, first : first + total.shape[1]] = total.astype(BF)
    lanes = iota((B, EXTRA), 1).astype(F32)
    meta = xm[own, :, D:].astype(F32)
    for k in range(top):
        hit = jnp.broadcast_to(meta[:, k : k + 1], (B, EXTRA)) == lanes
        value = jnp.sum(jnp.where(hit, scores, 0.0), axis=1, keepdims=True)
        gp_ref[:, k : k + 1] = value / meta[:, 8 + k : 9 + k]

    for piece in range(2):
        for way in range(2):
            for i in range(last[way] + 1):
                ag(way, i, piece).wait_send()
    for i in range(2):
        wx(i).wait_send()
    wg.wait_send()
    for n in range(4):
        for piece in range(2):
            for i in range(1, G):
                ip(n, piece, i, ahead[i], s).wait_send()
    for ch in range(2):
        for p in range(len(pieces[ch])):
            for i in range(1, G):
                rt(ch, p, i, ahead[i], s).wait_send()
    for p in range(len(spans)):
        for i in range(len(NEAR)):
            near(i, p).wait_send()
        for i in range(len(FAR)):
            far(i, p).wait_send()
        for i in range(len(LAST)):
            final(i, p).wait_send()


def body(tokens, out_grads, route_ids, route_probs, w_gate_up, w_down):
    B, D = tokens.shape
    top = route_ids.shape[1]
    H = w_down.shape[1]
    G = lax.axis_size("seq")
    Z = lax.axis_size("expert") // 2
    half = Z // 2
    quarter = Z // 4
    rows = G * quarter * CAP
    nt = quarter * B
    W2 = D + EXTRA
    pieces = (((0, D // 2), (D // 2, D // 2 + EXTRA)),) * 2
    count = max(len(p) for p in pieces)
    vmem = pl.BlockSpec(memory_space=pltpu.VMEM)
    anys = pl.BlockSpec(memory_space=pl.ANY)
    dma = pltpu.SemaphoreType.DMA
    held = (
        pltpu.VMEM((B, D), BF),
        pltpu.VMEM((B, top), F32),
        pltpu.VMEM(w_gate_up.shape, BF),
        pltpu.VMEM(w_down.shape, BF),
    )
    gt, gp, ggu, gd = pl.pallas_call(
        functools.partial(kernel, G, Z, top, pieces),
        out_shape=held,
        in_specs=[vmem, vmem, vmem, vmem, anys, anys],
        out_specs=(vmem,) * 4,
        scratch_shapes=[
            pltpu.VMEM((Z, B, W2), BF),
            pltpu.VMEM((Z, B, D), BF),
            pltpu.VMEM((2, 2, 2, rows, D), BF),
            pltpu.VMEM((2, 2, 2, rows, D), BF),
            pltpu.VMEM((4, nt, rows), BF),
            pltpu.VMEM((2, 2, H, D), BF),
            pltpu.VMEM((2, H, D), BF),
            pltpu.VMEM((2, 2, 2 * H, 2 * rows), BF),
            pltpu.VMEM((2, 2, H, 2 * rows), BF),
            pltpu.VMEM((2, 2, rows, W2), BF),
            pltpu.VMEM((2, 2, rows, W2), BF),
            pltpu.VMEM((Z, B, W2), F32),
            pltpu.VMEM((len(NEAR), B, W2), BF),
            pltpu.VMEM((len(NEAR), B, W2), BF),
            pltpu.VMEM((len(FAR), B, W2), BF),
            pltpu.VMEM((len(FAR), B, W2), BF),
            pltpu.VMEM((len(LAST), B, W2), BF),
            pltpu.VMEM((len(LAST), B, W2), BF),
            pltpu.VMEM((3 * H, D), F32),
            pltpu.VMEM((3 * H, D), F32),
            pltpu.VMEM((3 * H, D), F32),
            dma((2, 2, half)),
            dma((2, 2, half)),
            dma((4, 2, G)),
            dma((4, 2, G)),
            dma((2, count, G)),
            dma((2, count, G)),
            dma((len(NEAR), count)),
            dma((len(NEAR), count)),
            dma((len(FAR), count)),
            dma((len(FAR), count)),
            dma((len(LAST), count)),
            dma((len(LAST), count)),
            dma((3,)),
            dma((3,)),
            dma((2,)),
        ],
        compiler_params=pltpu.CompilerParams(
            collective_id=0, has_side_effects=True, vmem_limit_bytes=56 * 1024 * 1024
        ),
        name="moe_backward",
    )(tokens, out_grads, route_ids.T, route_probs.T, w_gate_up, w_down)
    return gt, gp, ggu, gd


def solution(mesh):
    in_specs = (
        P(("seq", "expert"), None),
        P(("seq", "expert"), None),
        P(("seq", "expert"), None),
        P(("seq", "expert"), None),
        P(("seq", "expert"), None, None, None),
        P(("seq", "expert"), None, None),
    )
    out_specs = (
        P(("seq", "expert"), None),
        P(("seq", "expert"), None),
        P(("seq", "expert"), None, None, None),
        P(("seq", "expert"), None, None),
    )
    return jax.shard_map(body, mesh=mesh, in_specs=in_specs, out_specs=out_specs, check_vma=False)
```
